256 devices in a mesh: lat: 16 (over x_lo, z), lon: 16 (over y, x_hi, core).
Axes of the slice: x: 4 (x_hi: 2, x_lo: 2; x = x_hi * 2 + x_lo), y: 4, z: 8, core: 2. Of those that a mesh axis runs over, the one named last changes fastest.
Arguments:
- field_in: bfloat16 [160, 1536, 512], P('lat', 'lon'), may hold values from -6 to 6
- kernel_taps: bfloat16 [3, 160, 3, 33], P(None, 'lat'), may hold values from -0.8984375 to 0.8984375
- row_reach: int32 [160], P('lat'), may hold values from 1 to 16, as said below
- mix_weight: bfloat16 [3, 512, 512], replicated, may hold values from -0.15625 to 0.15625
- up_weight: bfloat16 [512, 1024], replicated, may hold values from -0.25 to 0.25
- down_weight: bfloat16 [1024, 512], replicated, may hold values from -0.1875 to 0.1875
- cotangent: bfloat16 [160, 1536, 512], P('lat', 'lon'), may hold values from -6 to 6
Outputs:
- block_out: bfloat16 [160, 1536, 512], P('lat', 'lon')
- grad_field: bfloat16 [160, 1536, 512], P('lat', 'lon')
- grad_mix: bfloat16 [3, 512, 512], replicated
- grad_up: bfloat16 [512, 1024], replicated
- grad_down: bfloat16 [1024, 512], replicated
The draws below stay inside these ranges and needn't reach their ends.
Inputs may be any that keep to these rules, and one draw needn't show every extreme that they name: `row_reach`: how many longitude cells each latitude row's kernel reaches on either side.
All inputs are finite; a program needn't handle non-finite values.
Results may differ from the reference program's by a relative error of at most 0.0068.
Values may be sent and summed in bfloat16 or wider, within the bound.
A program may use at most 128 MiB of HBM per device.

```python
import jax
import jax.numpy as jnp
from jax import lax

C = 512
F = 1024
K = 3
HMAX = 16
ROWS_DEV = 10
TAPS = 33
NLAT = 160
NLON = 1536
POINTS = 245760


def draw_row_reach(key, part):
    rows_all = jnp.arange(NLAT, dtype=jnp.int32)
    pole_gap = jnp.minimum(rows_all, NLAT - 1 - rows_all)
    jitter = jax.random.randint(key, (NLAT,), 0, 3, dtype=jnp.int32)
    widen = HMAX * ROWS_DEV // (pole_gap + ROWS_DEV)
    spread = jnp.clip(widen - jitter, 1, HMAX)
    return jnp.where(pole_gap == 0, HMAX, spread).astype(jnp.int32)


def level_of(own_key, dims, split, least, high):
    level, own = 1.0, jax.random.fold_in(own_key, 6)
    for position, blocks in split:
        draws = jnp.exp(jax.random.uniform(jax.random.fold_in(own, position), (blocks,), jnp.float32, least / len(split), high / len(split)))
        level = level * jnp.repeat(draws, dims[position] // blocks).reshape([-1 if axis == position else 1 for axis in range(len(dims))])
    return level


def centred(rng, extent, scale, bound, split=(), kind=jnp.bfloat16):
    drawn = scale * jax.random.normal(rng, extent, jnp.float32)
    if split:
        drawn = drawn * level_of(rng, extent, split, -0.22, 0.18)
    return jnp.clip(drawn, -bound, bound).astype(kind)


def setup_inputs(seed: int = 0) -> dict:
    splits = jax.random.split(jax.random.key(seed), 8)
    field_in = centred(splits[0], (NLAT, NLON, C), 1.0, 6.0, ((0, 16), (1, 16)))
    kernel_taps = centred(splits[1], (K, NLAT, 3, TAPS), 0.15, 0.8984375, ((1, 16),))
    row_reach = draw_row_reach(jax.random.fold_in(splits[7], 71), 0)
    mix_weight = centred(splits[3], (K, C, C), (K * C) ** -0.5, 0.15625)
    up_weight = centred(splits[4], (C, F), C ** -0.5, 0.25)
    down_weight = centred(splits[5], (F, C), F ** -0.5, 0.1875)
    cotangent = centred(splits[6], (NLAT, NLON, C), 1.0, 6.0, ((0, 16), (1, 16)))
    return dict(field_in=field_in, kernel_taps=kernel_taps, row_reach=row_reach, mix_weight=mix_weight, up_weight=up_weight, down_weight=down_weight, cotangent=cotangent)


inv_root_two = 0.7071067811865476
inv_root_tau = 0.3989422804014327

def gelu_exact(value):
    return 0.5 * value * (1.0 + jax.scipy.special.erf(value * inv_root_two))

def gelu_slope(value):
    return 0.5 * (1.0 + jax.scipy.special.erf(value * inv_root_two)) + value * jnp.exp(-0.5 * value * value) * inv_root_tau

def features_of(field, kernel_taps, row_reach):
    offsets = jnp.arange(TAPS, dtype=jnp.int32) - HMAX
    col_index = (jnp.arange(NLON, dtype=jnp.int32)[:, None] + offsets[None, :]) % NLON
    north_row = jnp.roll(field[0], -(NLON // 2), axis=0)
    south_row = jnp.roll(field[NLAT - 1], -(NLON // 2), axis=0)
    padded = jnp.concatenate([north_row[None], field, south_row[None]], axis=0)
    tap_mask = jnp.abs(offsets)[None, :] <= row_reach[:, None]
    weights = jnp.where(tap_mask[None, :, None, :], kernel_taps.astype(jnp.float32), jnp.zeros((), jnp.float32))

    def one_row(index):
        three = lax.dynamic_slice_in_dim(padded, index, 3, 0)
        windows = three[:, col_index]
        row_taps = lax.dynamic_index_in_dim(weights, index, 1, keepdims=False)
        return jnp.einsum('kdt,djtc->kjc', row_taps, windows, precision=lax.Precision.HIGHEST)
    return lax.map(one_row, jnp.arange(NLAT, dtype=jnp.int32))

def reference(field_in, kernel_taps, row_reach, mix_weight, up_weight, down_weight, cotangent):
    features = features_of(field_in.astype(jnp.float32), kernel_taps, row_reach).astype(jnp.bfloat16)
    flat_features = jnp.transpose(features, (1, 0, 2, 3)).reshape(K, POINTS, C)
    flat_field = field_in.reshape(POINTS, C)
    conv_sum = jnp.zeros((POINTS, C), jnp.float32)
    for basis in range(K):
        conv_sum = conv_sum + jnp.dot(flat_features[basis], mix_weight[basis], preferred_element_type=jnp.float32)
    hidden = (flat_field.astype(jnp.float32) + conv_sum).astype(jnp.bfloat16)
    pre_act = jnp.dot(hidden, up_weight, preferred_element_type=jnp.float32)
    activated = gelu_exact(pre_act).astype(jnp.bfloat16)
    block_out = (hidden.astype(jnp.float32) + jnp.dot(activated, down_weight, preferred_element_type=jnp.float32)).astype(jnp.bfloat16)
    grad_rows = cotangent.reshape(POINTS, C)
    act_grad = jnp.dot(grad_rows, down_weight.T, preferred_element_type=jnp.float32)
    pre_grad = (act_grad * gelu_slope(pre_act)).astype(jnp.bfloat16)
    grad_scale = 1.0 / jnp.sqrt(jnp.float32(POINTS))
    grad_down = (jnp.dot(activated.T, grad_rows, preferred_element_type=jnp.float32) * grad_scale).astype(jnp.bfloat16)
    grad_up = (jnp.dot(hidden.T, pre_grad, preferred_element_type=jnp.float32) * grad_scale).astype(jnp.bfloat16)
    hidden_grad = (grad_rows.astype(jnp.float32) + jnp.dot(pre_grad, up_weight.T, preferred_element_type=jnp.float32)).astype(jnp.bfloat16)
    mix_parts = []
    feat_parts = []
    for basis in range(K):
        mix_parts.append(jnp.dot(flat_features[basis].T, hidden_grad, preferred_element_type=jnp.float32) * grad_scale)
        feat_parts.append(jnp.dot(hidden_grad, mix_weight[basis].T, preferred_element_type=jnp.float32).astype(jnp.bfloat16))
    grad_mix = jnp.stack(mix_parts).astype(jnp.bfloat16)
    feat_grad = jnp.stack(feat_parts).reshape(K, NLAT, NLON, C)
    feat_grad_rows = jnp.transpose(feat_grad, (1, 0, 2, 3)).astype(jnp.float32)
    unused, pullback = jax.vjp(lambda value: features_of(value, kernel_taps, row_reach), field_in.astype(jnp.float32))
    adjoint = pullback(feat_grad_rows)[0]
    grad_field = (hidden_grad.astype(jnp.float32).reshape(NLAT, NLON, C) + adjoint).astype(jnp.bfloat16)
    return (block_out.reshape(NLAT, NLON, C), grad_field, grad_mix, grad_up, grad_down)
```

```python
import math

import jax
import jax.numpy as jnp
from jax import lax
from jax.experimental import pallas as pl
from jax.experimental.pallas import tpu as pltpu
from jax.sharding import PartitionSpec as P

inv_root_two = 0.7071067811865476
inv_root_tau = 0.3989422804014327


MESH = pl.DeviceIdType.MESH
ring_xy = 4
ring_z = 8
lanes = 512


def multiple(value, of):
    return pl.multiple_of(value, of)


def remote(src, dst, send_sem, recv_sem, device):
    return pltpu.make_async_remote_copy(
        src_ref=src, dst_ref=dst, send_sem=send_sem, recv_sem=recv_sem, device_id=device, device_id_type=MESH
    )


class Place:
    def __init__(self):
        self.lat = lax.axis_index("lat")
        self.lon = lax.axis_index("lon")
        self.z = lax.rem(self.lat, ring_z)
        self.core = lax.rem(self.lon, 2)
        self.y = lax.div(self.lon, 4)
        self.x = lax.rem(lax.div(self.lon, 2), 2) * 2 + lax.div(self.lat, ring_z)
        self.first = self.x * (1 - self.core) + self.y * self.core
        self.second = self.y * (1 - self.core) + self.x * self.core

    def device(self, x, y, z, core):
        return (lax.rem(x, 2) * ring_z + z, y * 4 + lax.div(x, 2) * 2 + core)

    def partner(self):
        return self.device(self.x, self.y, self.z, 1 - self.core)

    def along_x(self, step):
        return self.device(lax.rem(self.x + step, ring_xy), self.y, self.z, self.core)

    def along_y(self, step):
        return self.device(self.x, lax.rem(self.y + step, ring_xy), self.z, self.core)

    def along_z(self, step):
        return self.device(self.x, self.y, lax.rem(self.z + step, ring_z), self.core)

    def along_first(self, step):
        x = lax.rem(self.x + step * (1 - self.core), ring_xy)
        y = lax.rem(self.y + step * self.core, ring_xy)
        return self.device(x, y, self.z, self.core)

    def along_second(self, step):
        x = lax.rem(self.x + step * self.core, ring_xy)
        y = lax.rem(self.y + step * (1 - self.core), ring_xy)
        return self.device(x, y, self.z, self.core)

    def everyone(self):
        found = [self.partner()]
        found += [self.along_x(s) for s in range(1, ring_xy)]
        found += [self.along_y(s) for s in range(1, ring_xy)]
        found += [self.along_z(s) for s in range(1, ring_z)]
        return found


def add_rows(dst, dst_at, sources, count, chunk):
    def body(i, carry):
        total = None
        for ref, at in sources:
            term = ref[pl.ds(multiple(at + i * chunk, 16), chunk), :].astype(jnp.float32)
            total = term if total is None else total + term
        dst[pl.ds(multiple(dst_at + i * chunk, 16), chunk), :] = total.astype(dst.dtype)
        return carry

    lax.fori_loop(0, count // chunk, body, 0)


wire_steps = (2, 1, 3)
z_steps = (4, 3, 5, 2, 6, 1, 7)


class Reduction:
    def __init__(self, place, rows, grad, out, parts, send, recv, scale):
        self.p = place
        self.rows = rows
        self.half, self.quarter, self.piece = rows // 2, rows // 8, rows // 32
        self.grad, self.out, self.scale = grad, out, scale
        self.r0, self.s0, self.r1, self.s1, self.r2, self.s2, self.r3, self.zbuf = parts
        self.send, self.recv = send, recv
        self.used = 0
        self.sent = []

    @staticmethod
    def scratch(rows):
        half, quarter, piece = rows // 2, rows // 8, rows // 32
        shapes = [
            (half, lanes), (half, lanes), (3, quarter, lanes), (quarter, lanes),
            (3, piece, lanes), (64, lanes), (7, 16, 256), (64, lanes),
        ]
        return [pltpu.VMEM(s, jnp.bfloat16) for s in shapes]

    def go(self, src, dst, device):
        copy = remote(src, dst, self.send.at[self.used], self.recv.at[self.used], device)
        self.used += 1
        copy.start()
        self.sent.append(copy)
        return copy

    def start_pair(self):
        p = self.p
        other = multiple((1 - p.core) * self.half, 16)
        self.flight = [self.go(self.grad.at[pl.ds(other, self.half), :], self.r0, p.partner())]

    def arrived(self):
        for copy in self.flight:
            copy.wait_recv()
        self.flight = []

    def pair_then_first(self):
        p = self.p
        self.arrived()
        flight = []
        for step in (2, 1, 3, 0):
            at = lax.rem(p.first + step, ring_xy) * self.quarter
            add_rows(self.s0, at, [(self.grad, p.core * self.half + at), (self.r0, at)], self.quarter, 32)
            if step:
                src = self.s0.at[pl.ds(multiple(at, 16), self.quarter), :]
                flight.append(self.go(src, self.r1.at[step - 1], p.along_first(step)))
        self.flight = flight

    def first_then_second(self):
        p = self.p
        self.arrived()
        flight = []
        own = p.first * self.quarter
        for step in (2, 1, 3, 0):
            at = lax.rem(p.second + step, ring_xy) * self.piece
            sources = [(self.s0, own + at)] + [(self.r1.at[i], at) for i in range(3)]
            add_rows(self.s1, at, sources, self.piece, 16)
            if step:
                src = self.s1.at[pl.ds(multiple(at, 16), self.piece), :]
                flight.append(self.go(src, self.r2.at[step - 1], p.along_second(step)))
        self.flight = flight

    def spot(self, ref, index):
        row = multiple(lax.div(index, 2) * 16, 16)
        lane = multiple(lax.rem(index, 2) * 256, 256)
        return ref.at[pl.ds(row, 16), pl.ds(lane, 256)]

    def second_then_z(self):
        p = self.p
        self.arrived()
        sources = [(self.s1, p.second * self.piece)] + [(self.r2.at[i], 0) for i in range(3)]
        add_rows(self.s2, 0, sources, self.piece, 16)
        if self.piece < 64:
            self.s2[self.piece :, :] = jnp.zeros((64 - self.piece, lanes), jnp.bfloat16)
        flight = []
        for step in z_steps:
            src = self.spot(self.s2, lax.rem(p.z + step, ring_z))
            flight.append(self.go(src, self.r3.at[step - 1], p.along_z(step)))
        self.flight = flight

    def z_then_back(self):
        p = self.p
        self.arrived()
        total = self.spot(self.s2, p.z)[...].astype(jnp.float32)
        for i in range(7):
            total = total + self.r3[i].astype(jnp.float32)
        mine = self.spot(self.zbuf, p.z)
        mine[...] = (total * self.scale).astype(jnp.bfloat16)
        self.flight = [self.go(mine, mine, p.along_z(step)) for step in z_steps]

    def back_second(self):
        p = self.p
        self.arrived()
        at = p.core * self.half + p.first * self.quarter + p.second * self.piece
        mine = self.out.at[pl.ds(multiple(at, 16), self.piece), :]
        mine[...] = self.zbuf[: self.piece, :]
        self.flight = [self.go(mine, mine, p.along_second(step)) for step in wire_steps]

    def back_first(self):
        p = self.p
        self.arrived()
        at = p.core * self.half + p.first * self.quarter
        mine = self.out.at[pl.ds(multiple(at, 16), self.quarter), :]
        self.flight = [self.go(mine, mine, p.along_first(step)) for step in wire_steps]

    def back_pair(self):
        p = self.p
        self.arrived()
        mine = self.out.at[pl.ds(multiple(p.core * self.half, 16), self.half), :]
        self.flight = [self.go(mine, mine, p.partner())]

    def finish(self):
        self.arrived()
        for copy in self.sent:
            copy.wait_send()


copies_each = 28


def meet(devices):
    barrier = pltpu.get_barrier_semaphore()
    for device in devices:
        pl.semaphore_signal(barrier, inc=1, device_id=device, device_id_type=MESH)
    pl.semaphore_wait(barrier, len(devices))


def sum_kernel(scale, mlp_ref, mix_ref, mlp_out, mix_out, *rest):
    place = Place()
    parts, sems = rest[:16], rest[16:]
    meet(place.everyone())
    mlp = Reduction(place, mlp_ref.shape[0], mlp_ref, mlp_out, parts[:8], sems[0], sems[1], scale)
    mix = Reduction(place, mix_ref.shape[0], mix_ref, mix_out, parts[8:], sems[2], sems[3], scale)
    both = (mlp, mix)
    for stage in (
        "start_pair", "pair_then_first", "first_then_second", "second_then_z", "z_then_back",
        "back_second", "back_first", "back_pair", "finish",
    ):
        for item in both:
            getattr(item, stage)()


def sum_everywhere(mlp, mix, scale):
    whole = pl.BlockSpec(memory_space=pltpu.VMEM)
    return pl.pallas_call(
        lambda *refs: sum_kernel(scale, *refs),
        out_shape=(
            jax.ShapeDtypeStruct(mlp.shape, jnp.bfloat16),
            jax.ShapeDtypeStruct(mix.shape, jnp.bfloat16),
        ),
        in_specs=[whole, whole],
        out_specs=(whole, whole),
        scratch_shapes=Reduction.scratch(mlp.shape[0])
        + Reduction.scratch(mix.shape[0])
        + [pltpu.SemaphoreType.DMA((copies_each,)) for _ in range(4)],
        compiler_params=pltpu.CompilerParams(
            collective_id=0, has_side_effects=True, vmem_limit_bytes=60 * 1024 * 1024
        ),
        name="weight_sums",
    )(mlp, mix)


def extended_2(x, sides, width, wrap):
    for axis, dim in sides:
        devices, length = (lax.axis_size(axis), x.shape[dim])
        up = [(i, (i + 1) % devices) for i in range(devices if wrap else devices - 1)]
        down = [(j, i) for i, j in up]
        last = lax.slice_in_dim(x, length - width, length, axis=dim)
        leading = lax.slice_in_dim(x, 0, width, axis=dim)
        before = lax.ppermute(last, axis, up)
        after = lax.ppermute(leading, axis, down)
        x = jnp.concatenate([before, x, after], axis=dim)
    return x


def shifted(block, axis, distance):
    devices = range(lax.axis_size(axis))
    route = [((i - distance) % len(devices), i) for i in devices]
    return lax.ppermute(block, axis, route)


def gelu_exact(value):
    return 0.5 * value * (1.0 + jax.scipy.special.erf(value * inv_root_two))


def gelu_slope(value):
    return (
        0.5 * (1.0 + jax.scipy.special.erf(value * inv_root_two))
        + value * jnp.exp(-0.5 * value * value) * inv_root_tau
    )


def local(field_in, kernel_taps, row_reach, mix_weight, up_weight, down_weight, cotangent):
    lat_rows, lon_cols, channels = field_in.shape
    basis_count = kernel_taps.shape[0]
    tap_count = kernel_taps.shape[3]
    reach_cells = (tap_count - 1) // 2
    lat_count = lax.axis_size("lat")
    lon_count = lax.axis_size("lon")
    lat_place = lax.axis_index("lat")
    north_pole = lat_place == 0
    south_pole = lat_place == lat_count - 1
    first_pass = extended_2(field_in, (("lat", 0),), 1, False)
    extended = extended_2(first_pass, (("lon", 1),), reach_cells, True)
    across = shifted(jnp.stack([extended[1], extended[lat_rows]]), "lon", lon_count // 2)
    extended = extended.at[0].set(jnp.where(north_pole, across[0], extended[0]))
    extended = extended.at[lat_rows + 1].set(
        jnp.where(south_pole, across[1], extended[lat_rows + 1])
    )
    padded_width = lon_cols + 2 * reach_cells
    offsets = jnp.arange(tap_count, dtype=jnp.int32) - reach_cells
    tap_mask = jnp.abs(offsets)[None, :] <= row_reach[:, None]
    masked_taps = jnp.where(
        tap_mask[None, :, None, :], kernel_taps, jnp.zeros((), kernel_taps.dtype)
    )
    selector = (
        jnp.arange(padded_width, dtype=jnp.int32)[None, :, None]
        - jnp.arange(lon_cols, dtype=jnp.int32)[:, None, None]
        == jnp.arange(tap_count, dtype=jnp.int32)[None, None, :]
    ).astype(jnp.bfloat16)
    band_matrix = jnp.einsum(
        "krdt,jat->krjda", masked_taps, selector, preferred_element_type=jnp.float32
    ).astype(jnp.bfloat16)
    windows = jnp.stack(
        [extended[0:lat_rows], extended[1 : lat_rows + 1], extended[2 : lat_rows + 2]], axis=1
    )
    features = jnp.einsum(
        "krjda,rdac->krjc", band_matrix, windows, preferred_element_type=jnp.float32
    ).astype(jnp.bfloat16)
    points = lat_rows * lon_cols
    flat_features = features.reshape(basis_count, points, channels)
    flat_field = field_in.reshape(points, channels)
    conv_sum = jnp.einsum(
        "kpc,kcd->pd", flat_features, mix_weight, preferred_element_type=jnp.float32
    )
    hidden = (flat_field.astype(jnp.float32) + conv_sum).astype(jnp.bfloat16)
    pre_act = jnp.dot(hidden, up_weight, preferred_element_type=jnp.float32)
    activated = gelu_exact(pre_act).astype(jnp.bfloat16)
    block_out = (
        hidden.astype(jnp.float32)
        + jnp.dot(activated, down_weight, preferred_element_type=jnp.float32)
    ).astype(jnp.bfloat16)
    grad_rows = cotangent.reshape(points, channels)
    act_grad = lax.dot_general(
        grad_rows, down_weight, (((1,), (1,)), ((), ())), preferred_element_type=jnp.float32
    )
    pre_grad = (act_grad * gelu_slope(pre_act)).astype(jnp.bfloat16)
    down_local = lax.dot_general(
        activated, grad_rows, (((0,), (0,)), ((), ())), preferred_element_type=jnp.float32
    )
    up_local = lax.dot_general(
        hidden, pre_grad, (((0,), (0,)), ((), ())), preferred_element_type=jnp.float32
    )
    hidden_grad = (
        grad_rows.astype(jnp.float32)
        + lax.dot_general(
            pre_grad, up_weight, (((1,), (1,)), ((), ())), preferred_element_type=jnp.float32
        )
    ).astype(jnp.bfloat16)
    mix_local = jnp.einsum(
        "kpc,pd->kcd", flat_features, hidden_grad, preferred_element_type=jnp.float32
    )
    feat_grad = jnp.einsum(
        "pd,kcd->kpc", hidden_grad, mix_weight, preferred_element_type=jnp.float32
    ).astype(jnp.bfloat16)
    feat_grad_rows = feat_grad.reshape(basis_count, lat_rows, lon_cols, channels)
    spread = jnp.einsum(
        "krjda,krjc->rdac", band_matrix, feat_grad_rows, preferred_element_type=jnp.float32
    )
    pulled = (
        jnp.pad(spread[:, 0], ((0, 2), (0, 0), (0, 0)))
        + jnp.pad(spread[:, 1], ((1, 1), (0, 0), (0, 0)))
        + jnp.pad(spread[:, 2], ((2, 0), (0, 0), (0, 0)))
    )
    returned = shifted(
        jnp.stack([pulled[0], pulled[lat_rows + 1]]).astype(jnp.bfloat16), "lon", lon_count // 2
    ).astype(jnp.float32)
    pulled = pulled.at[1].add(jnp.where(north_pole, returned[0], jnp.zeros_like(returned[0])))
    pulled = pulled.at[lat_rows].add(
        jnp.where(south_pole, returned[1], jnp.zeros_like(returned[1]))
    )
    col_rims = jnp.concatenate(
        [pulled[:, :reach_cells], pulled[:, lon_cols + reach_cells :]], axis=1
    )
    col_edges = extended_2(col_rims.astype(jnp.bfloat16), (("lon", 1),), reach_cells, True).astype(
        col_rims.dtype
    )
    interior = pulled[:, reach_cells : reach_cells + lon_cols]
    interior = interior.at[:, :reach_cells].add(col_edges[:, :reach_cells])
    interior = interior.at[:, lon_cols - reach_cells :].add(col_edges[:, 3 * reach_cells :])
    row_edges = extended_2(
        jnp.stack([interior[0], interior[lat_rows + 1]]).astype(jnp.bfloat16),
        (("lat", 0),),
        1,
        False,
    ).astype(jnp.float32)
    adjoint = interior[1 : lat_rows + 1]
    adjoint = adjoint.at[0].add(row_edges[0])
    adjoint = adjoint.at[lat_rows - 1].add(row_edges[3])
    grad_field = (
        hidden_grad.astype(jnp.float32).reshape(lat_rows, lon_cols, channels) + adjoint
    ).astype(jnp.bfloat16)
    grad_scale = 1.0 / math.sqrt(points * lat_count * lon_count)
    mlp_rows = jnp.concatenate(
        [up_local[:, :channels], up_local[:, channels:], down_local], axis=0
    ).astype(jnp.bfloat16)
    mix_rows = mix_local.astype(jnp.bfloat16).reshape(basis_count * channels, channels)
    mlp_out, mix_out = sum_everywhere(mlp_rows, mix_rows, grad_scale)
    up_out = jnp.concatenate([mlp_out[:channels], mlp_out[channels : 2 * channels]], axis=1)
    down_out = mlp_out[2 * channels :]
    mix_out = mix_out.reshape(basis_count, channels, channels)
    return (block_out.reshape(lat_rows, lon_cols, channels), grad_field, mix_out, up_out, down_out)


def solution(mesh):
    placed = (
        P("lat", "lon", None),
        P(None, "lat", None, None),
        P("lat"),
        P(),
        P(),
        P(),
        P("lat", "lon", None),
    )
    return jax.shard_map(
        local,
        mesh=mesh,
        in_specs=placed,
        out_specs=(P("lat", "lon", None), P("lat", "lon", None), P(), P(), P()),
        check_vma=False,
    )
```

```python
import math

import jax
import jax.numpy as jnp
from jax import lax
from jax.experimental import pallas as pl
from jax.experimental.pallas import tpu as pltpu
from jax.sharding import PartitionSpec as P

inv_root_two = 0.7071067811865476
inv_root_tau = 0.3989422804014327

MESH = pl.DeviceIdType.MESH
ring_xy = 4
ring_z = 8
lanes = 512


def multiple(value, of):
    return pl.multiple_of(value, of)


def remote(src, dst, send_sem, recv_sem, device):
    return pltpu.make_async_remote_copy(
        src_ref=src, dst_ref=dst, send_sem=send_sem, recv_sem=recv_sem, device_id=device, device_id_type=MESH
    )


class Place:
    def __init__(self):
        self.lat = lax.axis_index("lat")
        self.lon = lax.axis_index("lon")
        self.z = lax.rem(self.lat, ring_z)
        self.core = lax.rem(self.lon, 2)
        self.y = lax.div(self.lon, 4)
        self.x = lax.rem(lax.div(self.lon, 2), 2) * 2 + lax.div(self.lat, ring_z)
        self.first = self.x * (1 - self.core) + self.y * self.core
        self.second = self.y * (1 - self.core) + self.x * self.core

    def device(self, x, y, z, core):
        return (lax.rem(x, 2) * ring_z + z, y * 4 + lax.div(x, 2) * 2 + core)

    def partner(self):
        return self.device(self.x, self.y, self.z, 1 - self.core)

    def along_x(self, step):
        return self.device(lax.rem(self.x + step, ring_xy), self.y, self.z, self.core)

    def along_y(self, step):
        return self.device(self.x, lax.rem(self.y + step, ring_xy), self.z, self.core)

    def along_z(self, step):
        return self.device(self.x, self.y, lax.rem(self.z + step, ring_z), self.core)

    def along_first(self, step):
        x = lax.rem(self.x + step * (1 - self.core), ring_xy)
        y = lax.rem(self.y + step * self.core, ring_xy)
        return self.device(x, y, self.z, self.core)

    def along_second(self, step):
        x = lax.rem(self.x + step * self.core, ring_xy)
        y = lax.rem(self.y + step * (1 - self.core), ring_xy)
        return self.device(x, y, self.z, self.core)

    def everyone(self):
        found = [self.partner()]
        found += [self.along_x(s) for s in range(1, ring_xy)]
        found += [self.along_y(s) for s in range(1, ring_xy)]
        found += [self.along_z(s) for s in range(1, ring_z)]
        return found


def add_rows(dst, dst_at, sources, count, chunk):
    def body(i, carry):
        total = None
        for ref, at in sources:
            term = ref[pl.ds(multiple(at + i * chunk, 16), chunk), :].astype(jnp.float32)
            total = term if total is None else total + term
        dst[pl.ds(multiple(dst_at + i * chunk, 16), chunk), :] = total.astype(dst.dtype)
        return carry

    lax.fori_loop(0, count // chunk, body, 0)


wire_steps = (2, 1, 3)
z_steps = (4, 3, 5, 2, 6, 1, 7)


class Reduction:
    def __init__(self, place, rows, grad, out, parts, send, recv, scale):
        self.p = place
        self.rows = rows
        self.half, self.quarter, self.piece = rows // 2, rows // 8, rows // 32
        self.grad, self.out, self.scale = grad, out, scale
        self.r0, self.s0, self.r1, self.s1, self.r2, self.s2, self.r3, self.zbuf = parts
        self.send, self.recv = send, recv
        self.used = 0
        self.sent = []

    @staticmethod
    def scratch(rows):
        half, quarter, piece = rows // 2, rows // 8, rows // 32
        shapes = [
            (half, lanes), (half, lanes), (3, quarter, lanes), (quarter, lanes),
            (3, piece, lanes), (64, lanes), (7, 16, 256), (64, lanes),
        ]
        return [pltpu.VMEM(s, jnp.bfloat16) for s in shapes]

    def go(self, src, dst, device):
        copy = remote(src, dst, self.send.at[self.used], self.recv.at[self.used], device)
        self.used += 1
        copy.start()
        self.sent.append(copy)
        return copy

    def start_pair(self):
        p = self.p
        other = multiple((1 - p.core) * self.half, 16)
        self.flight = [self.go(self.grad.at[pl.ds(other, self.half), :], self.r0, p.partner())]

    def arrived(self):
        for copy in self.flight:
            copy.wait_recv()
        self.flight = []

    def pair_then_first(self):
        p = self.p
        self.arrived()
        flight = []
        for step in (2, 1, 3, 0):
            at = lax.rem(p.first + step, ring_xy) * self.quarter
            add_rows(self.s0, at, [(self.grad, p.core * self.half + at), (self.r0, at)], self.quarter, 32)
            if step:
                src = self.s0.at[pl.ds(multiple(at, 16), self.quarter), :]
                flight.append(self.go(src, self.r1.at[step - 1], p.along_first(step)))
        self.flight = flight

    def first_then_second(self):
        p = self.p
        self.arrived()
        flight = []
        own = p.first * self.quarter
        for step in (2, 1, 3, 0):
            at = lax.rem(p.second + step, ring_xy) * self.piece
            sources = [(self.s0, own + at)] + [(self.r1.at[i], at) for i in range(3)]
            add_rows(self.s1, at, sources, self.piece, 16)
            if step:
                src = self.s1.at[pl.ds(multiple(at, 16), self.piece), :]
                flight.append(self.go(src, self.r2.at[step - 1], p.along_second(step)))
        self.flight = flight

    def spot(self, ref, index):
        row = multiple(lax.div(index, 2) * 16, 16)
        lane = multiple(lax.rem(index, 2) * 256, 256)
        return ref.at[pl.ds(row, 16), pl.ds(lane, 256)]

    def second_then_z(self):
        p = self.p
        self.arrived()
        sources = [(self.s1, p.second * self.piece)] + [(self.r2.at[i], 0) for i in range(3)]
        add_rows(self.s2, 0, sources, self.piece, 16)
        if self.piece < 64:
            self.s2[self.piece :, :] = jnp.zeros((64 - self.piece, lanes), jnp.bfloat16)
        flight = []
        for step in z_steps:
            src = self.spot(self.s2, lax.rem(p.z + step, ring_z))
            flight.append(self.go(src, self.r3.at[step - 1], p.along_z(step)))
        self.flight = flight

    def z_then_back(self):
        p = self.p
        self.arrived()
        total = self.spot(self.s2, p.z)[...].astype(jnp.float32)
        for i in range(7):
            total = total + self.r3[i].astype(jnp.float32)
        mine = self.spot(self.zbuf, p.z)
        mine[...] = (total * self.scale).astype(jnp.bfloat16)
        self.flight = [self.go(mine, mine, p.along_z(step)) for step in z_steps]

    def back_second(self):
        p = self.p
        self.arrived()
        at = p.core * self.half + p.first * self.quarter + p.second * self.piece
        mine = self.out.at[pl.ds(multiple(at, 16), self.piece), :]
        mine[...] = self.zbuf[: self.piece, :]
        self.flight = [self.go(mine, mine, p.along_second(step)) for step in wire_steps]

    def back_first(self):
        p = self.p
        self.arrived()
        at = p.core * self.half + p.first * self.quarter
        mine = self.out.at[pl.ds(multiple(at, 16), self.quarter), :]
        self.flight = [self.go(mine, mine, p.along_first(step)) for step in wire_steps]

    def back_pair(self):
        p = self.p
        self.arrived()
        mine = self.out.at[pl.ds(multiple(p.core * self.half, 16), self.half), :]
        self.flight = [self.go(mine, mine, p.partner())]

    def finish(self):
        self.arrived()
        for copy in self.sent:
            copy.wait_send()


copies_each = 28


rows = 10
cols = 96
reach = 16
wide = cols + 2 * reach
taps = 2 * reach + 1
basis = 3
points = rows * cols
hidden_units = 1024
chunk_rows = 2
chunk = chunk_rows * cols
chunks = rows // chunk_rows
span = basis * cols
depth = 3 * wide
f32 = jnp.float32
bf16 = jnp.bfloat16


def mm(a, b):
    return jnp.dot(a, b, preferred_element_type=f32)


def mm_nt(a, b):
    return lax.dot_general(a, b, (((1,), (1,)), ((), ())), preferred_element_type=f32)


def mm_tn(a, b):
    return lax.dot_general(a, b, (((0,), (0,)), ((), ())), preferred_element_type=f32)


class Halo:
    def __init__(self, place):
        lat, lon = place.lat, place.lon
        top = (lat == 0).astype(jnp.int32)
        bottom = (lat == 15).astype(jnp.int32)
        self.top, self.bottom = top, bottom
        self.lat, self.lon = lat, lon
        self.north = lat - 1 + top
        self.south = lat + 1 - bottom
        self.side_n = 1 - top
        self.side_s = bottom

    def upper(self, shift):
        return (self.north, lax.rem(self.lon + 16 + shift + 8 * self.top, 16))

    def lower(self, shift):
        return (self.south, lax.rem(self.lon + 16 + shift + 8 * self.bottom, 16))

    def beside(self, shift):
        return (self.lat, lax.rem(self.lon + 16 + shift, 16))

    def everyone(self):
        return [self.upper(s) for s in (0, -1, 1)] + [self.lower(s) for s in (0, -1, 1)] + [self.beside(-1), self.beside(1)]

    def send(self, ext, send, recv):
        own = slice(reach, reach + cols)
        first, last = slice(reach, 2 * reach), slice(cols, cols + reach)
        left, right = slice(0, reach), slice(reach + cols, wide)
        copies = []
        copies.append(remote(ext.at[1 : rows + 1, first], ext.at[1 : rows + 1, right], send.at[6], recv.at[6], self.beside(-1)))
        copies.append(remote(ext.at[1 : rows + 1, last], ext.at[1 : rows + 1, left], send.at[7], recv.at[7], self.beside(1)))
        for number, (side, target, row) in enumerate(((self.side_n, self.upper, 1), (self.side_s, self.lower, rows))):
            to = side * (rows + 1)
            plan = ((own, own, 0), (first, right, -1), (last, left, 1))
            for part, (src, dst, shift) in enumerate(plan):
                copies.append(
                    remote(
                        ext.at[row, src], ext.at[to, dst], send.at[number * 3 + part], recv.at[side * 3 + part], target(shift)
                    )
                )
        for copy in copies:
            copy.start()
        return copies

    def wait(self, ext, send, recv):
        own = slice(reach, reach + cols)
        left, right = slice(0, reach), slice(reach + cols, wide)
        me = self.beside(1)
        for side in range(2):
            for part, where in enumerate((own, right, left)):
                here = ext.at[side * (rows + 1), where]
                remote(here, here, send.at[0], recv.at[side * 3 + part], me).wait_recv()
        here = ext.at[1 : rows + 1, right]
        remote(here, here, send.at[0], recv.at[6], me).wait_recv()
        here = ext.at[1 : rows + 1, left]
        remote(here, here, send.at[0], recv.at[7], me).wait_recv()


def toeplitz(row):
    spread = jnp.broadcast_to(row, (cols, wide))
    return pltpu.roll(spread, 0, 1, stride=1, stride_axis=0).astype(bf16)


def step_kernel(
    scale,
    field_in, taps_in, mix_in, up_in, down_in, cot_in,
    block_out, field_out, mix_out, up_out, down_out,
    ext, gext, band, adjoint, tapx, feats, cot, hidden, act_grad, act, pre_grad, out_rows, mix, up, down,
    g_mlp, g_mix, t_mlp, t_mix,
    load_sem, store_sem, halo_send, halo_recv, grad_send, grad_recv, tap_send, tap_recv,
    *rest,
):
    place = Place()
    halo = Halo(place)
    own = slice(reach, reach + cols)

    loads = [
        pltpu.make_async_copy(taps_in, tapx.at[1 : rows + 1], load_sem.at[0]),
        pltpu.make_async_copy(field_in, ext.at[1 : rows + 1, own], load_sem.at[1]),
        pltpu.make_async_copy(cot_in, cot, load_sem.at[2]),
        pltpu.make_async_copy(down_in, down, load_sem.at[3]),
        pltpu.make_async_copy(mix_in, mix, load_sem.at[4]),
        pltpu.make_async_copy(up_in, up, load_sem.at[5]),
    ]
    for load in loads:
        load.start()
    devices = place.everyone() + halo.everyone()
    barrier = pltpu.get_barrier_semaphore()
    for device in devices:
        pl.semaphore_signal(barrier, inc=1, device_id=device, device_id_type=MESH)

    loads[0].wait()

    def build(r, carry):
        for k in range(basis):
            for d in range(3):
                band[r, k * cols : (k + 1) * cols, d * wide : (d + 1) * wide] = toeplitz(
                    tapx[r + 1, k * 3 + d : k * 3 + d + 1, :]
                )
        return carry

    lax.fori_loop(0, rows, build, 0)
    loads[1].wait()
    pl.semaphore_wait(barrier, len(devices))
    sent = halo.send(ext, halo_send, halo_recv)
    tap_copies = [
        remote(tapx.at[1], tapx.at[halo.side_n * (rows + 1)], tap_send.at[0], tap_recv.at[halo.side_n], halo.upper(0)),
        remote(tapx.at[rows], tapx.at[halo.side_s * (rows + 1)], tap_send.at[1], tap_recv.at[halo.side_s], halo.lower(0)),
    ]
    for copy in tap_copies:
        copy.start()
    sent += tap_copies

    loads[2].wait()
    loads[3].wait()

    def early(i, carry):
        at = pl.ds(multiple(i * chunk, 16), chunk)
        grad = cot[pl.ds(i * chunk_rows, chunk_rows)].reshape(chunk, lanes)
        act_grad[at, :] = mm_nt(grad, down[...])
        return carry

    lax.fori_loop(0, chunks, early, 0)

    def build_back(r, carry):
        for k in range(basis):
            for s in range(3):
                at = 9 + k * 3 + 2 - s
                adjoint[r, k * cols : (k + 1) * cols, s * wide : (s + 1) * wide] = toeplitz(tapx[r + s, at : at + 1, :])
        return carry

    lax.fori_loop(1, rows - 1, build_back, 0)

    loads[4].wait()
    loads[5].wait()
    halo.wait(ext, halo_send, halo_recv)

    def features(r, carry):
        window = ext[pl.ds(r, 3)].reshape(depth, lanes)
        made = mm(band[r], window).astype(bf16)
        at = pl.ds(multiple(r * cols, 16), cols)
        for k in range(basis):
            feats[k, at, :] = made[k * cols : (k + 1) * cols]
        return carry

    lax.fori_loop(0, rows, features, 0)

    def pointwise(i, carry):
        at = pl.ds(multiple(i * chunk, 16), chunk)
        total = ext[pl.ds(1 + i * chunk_rows, chunk_rows), own].reshape(chunk, lanes).astype(f32)
        for k in range(basis):
            total = total + mm(feats[k, at, :], mix[k])
        inner = total.astype(bf16)
        hidden[at, :] = inner
        for block in range(hidden_units // 256):
            f = slice(block * 256, (block + 1) * 256)
            value = mm(inner, up[:, f])
            cdf = 0.5 * (1.0 + lax.erf(value * inv_root_two))
            act[at, f] = (value * cdf).astype(bf16)
            slope = cdf + value * jnp.exp(-0.5 * value * value) * inv_root_tau
            pre_grad[at, f] = (act_grad[at, f] * slope).astype(bf16)
        made = (inner.astype(f32) + mm(act[at, :], down[...])).astype(bf16)
        out_rows[pl.ds(i * chunk_rows, chunk_rows)] = made.reshape(chunk_rows, cols, lanes)
        grad = cot[pl.ds(i * chunk_rows, chunk_rows)].reshape(chunk, lanes).astype(f32)
        grad = (grad + mm_nt(pre_grad[at, :], up[...])).astype(bf16)
        gext[pl.ds(1 + i * chunk_rows, chunk_rows), own] = grad.reshape(chunk_rows, cols, lanes)
        return carry

    lax.fori_loop(0, chunks, pointwise, 0)
    stores = [pltpu.make_async_copy(out_rows, block_out, store_sem.at[0])]
    stores[0].start()
    sent += halo.send(gext, grad_send, grad_recv)

    def flat(ref):
        return ref[...].reshape(points, lanes)

    def weight_down(i, carry):
        part = pl.ds(multiple(i * 256, 256), 256)
        g_mlp[pl.ds(multiple(1024 + i * 256, 256), 256), :] = mm_tn(act[:, part], flat(cot)).astype(bf16)
        return carry

    lax.fori_loop(0, 4, weight_down, 0)

    def weight_up(i, carry):
        part = pl.ds(multiple(i * 256, 256), 256)
        left = hidden[:, part]
        for side in range(2):
            g_mlp[pl.ds(multiple(side * 512 + i * 256, 256), 256), :] = mm_tn(
                left, pre_grad[:, side * 512 : side * 512 + 512]
            ).astype(bf16)
        return carry

    lax.fori_loop(0, 2, weight_up, 0)

    mlp_sum = Reduction(place, 2048, g_mlp, t_mlp, rest[0:8], rest[16], rest[17], scale)
    mix_sum = Reduction(place, 1536, g_mix, t_mix, rest[8:16], rest[18], rest[19], scale)
    mlp_sum.start_pair()

    def weight_mix(i, carry):
        k, half = lax.div(i, 2), lax.rem(i, 2)
        part = pl.ds(multiple(half * 256, 256), 256)
        grad = gext[1 : rows + 1, own].reshape(points, lanes)
        g_mix[pl.ds(multiple(i * 256, 256), 256), :] = mm_tn(feats[k, :, part], grad).astype(bf16)
        return carry

    lax.fori_loop(0, 6, weight_mix, 0)
    mix_sum.start_pair()
    mlp_sum.pair_then_first()

    for side in range(2):
        here = tapx.at[side * (rows + 1)]
        remote(here, here, tap_send.at[0], tap_recv.at[side], halo.beside(1)).wait_recv()
    for r, pole in ((0, halo.top), (rows - 1, halo.bottom)):
        for k in range(basis):
            for s in range(3):
                at = 9 + k * 3 + 2 - s
                row = tapx[r + s, at : at + 1, :]
                if (r, s) == (0, 0) or (r, s) == (rows - 1, 2):
                    other = 9 + k * 3 + s
                    row = jnp.where(pole == 1, tapx[r + s, other : other + 1, :], row)
                adjoint[r, k * cols : (k + 1) * cols, s * wide : (s + 1) * wide] = toeplitz(row)
    halo.wait(gext, grad_send, grad_recv)

    def pull(r, carry):
        window = gext[pl.ds(r, 3)].reshape(depth, lanes)
        made = mm(adjoint[r], window).astype(bf16)
        at = pl.ds(multiple(r * cols, 16), cols)
        for k in range(basis):
            feats[k, at, :] = made[k * cols : (k + 1) * cols]
        return carry

    lax.fori_loop(0, rows, pull, 0)
    mix_sum.pair_then_first()
    stores[0].wait()

    def last(i, carry):
        at = pl.ds(multiple(i * chunk, 16), chunk)
        total = gext[pl.ds(1 + i * chunk_rows, chunk_rows), own].reshape(chunk, lanes).astype(f32)
        for k in range(basis):
            total = total + mm_nt(feats[k, at, :], mix[k])
        out_rows[pl.ds(i * chunk_rows, chunk_rows)] = total.astype(bf16).reshape(chunk_rows, cols, lanes)
        return carry

    lax.fori_loop(0, chunks, last, 0)
    stores = [pltpu.make_async_copy(out_rows, field_out, store_sem.at[1])]
    stores[0].start()

    for stage in ("first_then_second", "second_then_z", "z_then_back", "back_second", "back_first", "back_pair", "finish"):
        for item in (mlp_sum, mix_sum):
            getattr(item, stage)()
    stores.append(pltpu.make_async_copy(t_mlp.at[0:512], up_out.at[:, 0:512], store_sem.at[2]))
    stores.append(pltpu.make_async_copy(t_mlp.at[512:1024], up_out.at[:, 512:1024], store_sem.at[3]))
    stores.append(pltpu.make_async_copy(t_mlp.at[1024:2048], down_out, store_sem.at[4]))
    for k in range(basis):
        stores.append(pltpu.make_async_copy(t_mix.at[k * 512 : k * 512 + 512], mix_out.at[k], store_sem.at[5 + k]))
    for store in stores[1:]:
        store.start()
    for store in stores:
        store.wait()
    for copy in sent:
        copy.wait_send()


def local(field_in, kernel_taps, row_reach, mix_weight, up_weight, down_weight, cotangent):
    offsets = jnp.arange(taps, dtype=jnp.int32) - reach
    mask = jnp.abs(offsets)[None, :] <= row_reach[:, None]
    masked = jnp.where(mask[None, :, None, :], kernel_taps, jnp.zeros((), kernel_taps.dtype)).astype(f32)
    masked = jnp.transpose(masked, (1, 0, 2, 3)).reshape(rows, 9, taps)
    tap_rows = jnp.concatenate([masked, masked[:, :, ::-1]], axis=1)
    tap_rows = jnp.pad(tap_rows, ((0, 0), (0, 6), (0, wide - taps)))
    total_points = points * lax.axis_size("lat") * lax.axis_size("lon")
    scale = 1.0 / math.sqrt(total_points)
    anywhere = pl.BlockSpec(memory_space=pl.ANY)
    v = pltpu.VMEM
    dma = pltpu.SemaphoreType.DMA
    return pl.pallas_call(
        lambda *refs: step_kernel(scale, *refs),
        out_shape=(
            jax.ShapeDtypeStruct(field_in.shape, bf16),
            jax.ShapeDtypeStruct(field_in.shape, bf16),
            jax.ShapeDtypeStruct(mix_weight.shape, bf16),
            jax.ShapeDtypeStruct(up_weight.shape, bf16),
            jax.ShapeDtypeStruct(down_weight.shape, bf16),
        ),
        in_specs=[anywhere] * 6,
        out_specs=(anywhere,) * 5,
        scratch_shapes=[
            v((rows + 2, wide, lanes), bf16),
            v((rows + 2, wide, lanes), bf16),
            v((rows, span, depth), bf16),
            v((rows, span, depth), bf16),
            v((rows + 2, 24, wide), f32),
            v((basis, points, lanes), bf16),
            v((rows, cols, lanes), bf16),
            v((points, lanes), bf16),
            v((points, hidden_units), f32),
            v((points, hidden_units), bf16),
            v((points, hidden_units), bf16),
            v((rows, cols, lanes), bf16),
            v((basis, lanes, lanes), bf16),
            v((lanes, hidden_units), bf16),
            v((hidden_units, lanes), bf16),
            v((2048, lanes), bf16),
            v((1536, lanes), bf16),
            v((2048, lanes), bf16),
            v((1536, lanes), bf16),
            dma((6,)), dma((8,)), dma((8,)), dma((8,)), dma((8,)), dma((8,)), dma((2,)), dma((2,)),
        ]
        + Reduction.scratch(2048)
        + Reduction.scratch(1536)
        + [dma((copies_each,)) for _ in range(4)],
        compiler_params=pltpu.CompilerParams(
            collective_id=0, has_side_effects=True, vmem_limit_bytes=64000 * 1024
        ),
        name="disco_step",
    )(field_in, tap_rows, mix_weight, up_weight, down_weight, cotangent)


def solution(mesh):
    placed = (
        P("lat", "lon", None),
        P(None, "lat", None, None),
        P("lat"),
        P(),
        P(),
        P(),
        P("lat", "lon", None),
    )
    return jax.shard_map(
        local,
        mesh=mesh,
        in_specs=placed,
        out_specs=(P("lat", "lon", None), P("lat", "lon", None), P(), P(), P()),
        check_vma=False,
    )
```

```python
import math

import jax
import jax.numpy as jnp
from jax import lax
from jax.experimental import pallas as pl
from jax.experimental.pallas import tpu as pltpu
from jax.sharding import PartitionSpec as P

inv_root_two = 0.7071067811865476
inv_root_tau = 0.3989422804014327

MESH = pl.DeviceIdType.MESH
ring_xy = 4
ring_z = 8
lanes = 512


def multiple(value, of):
    return pl.multiple_of(value, of)


def remote(src, dst, send_sem, recv_sem, device):
    return pltpu.make_async_remote_copy(
        src_ref=src, dst_ref=dst, send_sem=send_sem, recv_sem=recv_sem, device_id=device, device_id_type=MESH
    )


class Place:
    def __init__(self):
        self.lat = lax.axis_index("lat")
        self.lon = lax.axis_index("lon")
        self.z = lax.rem(self.lat, ring_z)
        self.core = lax.rem(self.lon, 2)
        self.y = lax.div(self.lon, 4)
        self.x = lax.rem(lax.div(self.lon, 2), 2) * 2 + lax.div(self.lat, ring_z)
        self.first = self.x * (1 - self.core) + self.y * self.core
        self.second = self.y * (1 - self.core) + self.x * self.core

    def device(self, x, y, z, core):
        return (lax.rem(x, 2) * ring_z + z, y * 4 + lax.div(x, 2) * 2 + core)

    def partner(self):
        return self.device(self.x, self.y, self.z, 1 - self.core)

    def along_x(self, step):
        return self.device(lax.rem(self.x + step, ring_xy), self.y, self.z, self.core)

    def along_y(self, step):
        return self.device(self.x, lax.rem(self.y + step, ring_xy), self.z, self.core)

    def along_z(self, step):
        return self.device(self.x, self.y, lax.rem(self.z + step, ring_z), self.core)

    def along_first(self, step):
        x = lax.rem(self.x + step * (1 - self.core), ring_xy)
        y = lax.rem(self.y + step * self.core, ring_xy)
        return self.device(x, y, self.z, self.core)

    def along_second(self, step):
        x = lax.rem(self.x + step * self.core, ring_xy)
        y = lax.rem(self.y + step * (1 - self.core), ring_xy)
        return self.device(x, y, self.z, self.core)

    def everyone(self):
        found = [self.partner()]
        found += [self.along_x(s) for s in range(1, ring_xy)]
        found += [self.along_y(s) for s in range(1, ring_xy)]
        found += [self.along_z(s) for s in range(1, ring_z)]
        return found


def add_rows(dst, dst_at, sources, count, chunk):
    def body(i, carry):
        total = None
        for ref, at in sources:
            term = ref[pl.ds(multiple(at + i * chunk, 16), chunk), :].astype(jnp.float32)
            total = term if total is None else total + term
        dst[pl.ds(multiple(dst_at + i * chunk, 16), chunk), :] = total.astype(dst.dtype)
        return carry

    lax.fori_loop(0, count // chunk, body, 0)


wire_steps = (2, 1, 3)
z_steps = (4, 3, 5, 2, 6, 1, 7)


class Reduction:
    def __init__(self, place, start, rows, grad, out, parts, send, recv, scale):
        self.p = place
        self.half, self.quarter, self.piece = rows // 2, rows // 8, rows // 32
        self.grad, self.out, self.scale = grad.at[start : start + rows], out.at[start : start + rows], scale
        self.r0, self.s0, self.r1, self.s1, self.r2, self.s2, self.r3, self.zbuf = parts
        self.send, self.recv = send, recv
        self.used = 0
        self.sent = []

    @staticmethod
    def scratch(rows):
        half, quarter, piece = rows // 2, rows // 8, rows // 32
        shapes = [
            (half, lanes), (half, lanes), (3, quarter, lanes), (quarter, lanes),
            (3, piece, lanes), (32, lanes), (7, 16, 128), (32, lanes),
        ]
        return [pltpu.VMEM(s, jnp.bfloat16) for s in shapes]

    def go(self, src, dst, device):
        copy = remote(src, dst, self.send.at[self.used], self.recv.at[self.used], device)
        self.used += 1
        copy.start()
        self.sent.append(copy)
        return copy

    def start_pair(self):
        p = self.p
        other = multiple((1 - p.core) * self.half, 16)
        self.flight = [self.go(self.grad.at[pl.ds(other, self.half), :], self.r0, p.partner())]

    def arrived(self):
        for copy in self.flight:
            copy.wait_recv()
        self.flight = []

    def pair_then_first(self):
        p = self.p
        self.arrived()
        flight = []
        for step in (2, 1, 3, 0):
            at = lax.rem(p.first + step, ring_xy) * self.quarter
            add_rows(self.s0, at, [(self.grad, p.core * self.half + at), (self.r0, at)], self.quarter, 32)
            if step:
                src = self.s0.at[pl.ds(multiple(at, 16), self.quarter), :]
                flight.append(self.go(src, self.r1.at[step - 1], p.along_first(step)))
        self.flight = flight

    def first_then_second(self):
        p = self.p
        self.arrived()
        flight = []
        own = p.first * self.quarter
        for step in (2, 1, 3, 0):
            at = lax.rem(p.second + step, ring_xy) * self.piece
            sources = [(self.s0, own + at)] + [(self.r1.at[i], at) for i in range(3)]
            add_rows(self.s1, at, sources, self.piece, 16)
            if step:
                src = self.s1.at[pl.ds(multiple(at, 16), self.piece), :]
                flight.append(self.go(src, self.r2.at[step - 1], p.along_second(step)))
        self.flight = flight

    def spot(self, ref, index):
        row = multiple(lax.div(index, 4) * 16, 16)
        lane = multiple(lax.rem(index, 4) * 128, 128)
        return ref.at[pl.ds(row, 16), pl.ds(lane, 128)]

    def second_then_z(self):
        p = self.p
        self.arrived()
        sources = [(self.s1, p.second * self.piece)] + [(self.r2.at[i], 0) for i in range(3)]
        add_rows(self.s2, 0, sources, self.piece, 16)
        if self.piece < 32:
            self.s2[self.piece :, :] = jnp.zeros((32 - self.piece, lanes), jnp.bfloat16)
        flight = []
        for step in z_steps:
            src = self.spot(self.s2, lax.rem(p.z + step, ring_z))
            flight.append(self.go(src, self.r3.at[step - 1], p.along_z(step)))
        self.flight = flight

    def z_then_back(self):
        p = self.p
        self.arrived()
        total = self.spot(self.s2, p.z)[...].astype(jnp.float32)
        for i in range(7):
            total = total + self.r3[i].astype(jnp.float32)
        mine = self.spot(self.zbuf, p.z)
        mine[...] = (total * self.scale).astype(jnp.bfloat16)
        self.flight = [self.go(mine, mine, p.along_z(step)) for step in z_steps]

    def back_second(self):
        p = self.p
        self.arrived()
        at = p.core * self.half + p.first * self.quarter + p.second * self.piece
        mine = self.out.at[pl.ds(multiple(at, 16), self.piece), :]
        mine[...] = self.zbuf[: self.piece, :]
        self.flight = [self.go(mine, mine, p.along_second(step)) for step in wire_steps]

    def back_first(self):
        p = self.p
        self.arrived()
        at = p.core * self.half + p.first * self.quarter
        mine = self.out.at[pl.ds(multiple(at, 16), self.quarter), :]
        self.flight = [self.go(mine, mine, p.along_first(step)) for step in wire_steps]

    def back_pair(self):
        p = self.p
        self.arrived()
        mine = self.out.at[pl.ds(multiple(p.core * self.half, 16), self.half), :]
        self.flight = [self.go(mine, mine, p.partner())]

    def finish(self):
        self.arrived()
        for copy in self.sent:
            copy.wait_send()


copies_each = 28
stacks = ((0, 1024), (1024, 1024), (2048, 1024), (3072, 512))


rows = 10
cols = 96
reach = 16
vmem_room = 48 * 1024 * 1024
wide = cols + 2 * reach
taps = 2 * reach + 1
basis = 3
points = rows * cols
hidden_units = 1024
chunk_rows = 2
chunk = chunk_rows * cols
chunks = rows // chunk_rows
span = basis * cols
depth = 3 * wide
f32 = jnp.float32
bf16 = jnp.bfloat16


def mm(a, b):
    return jnp.dot(a, b, preferred_element_type=f32)


def mm_nt(a, b):
    return lax.dot_general(a, b, (((1,), (1,)), ((), ())), preferred_element_type=f32)


def mm_tn(a, b):
    return lax.dot_general(a, b, (((0,), (0,)), ((), ())), preferred_element_type=f32)


class Halo:
    def __init__(self, place):
        lat, lon = place.lat, place.lon
        top = (lat == 0).astype(jnp.int32)
        bottom = (lat == 15).astype(jnp.int32)
        self.top, self.bottom = top, bottom
        self.lat, self.lon = lat, lon
        self.north = lat - 1 + top
        self.south = lat + 1 - bottom
        self.side_n = 1 - top
        self.side_s = bottom

    def upper(self, shift):
        return (self.north, lax.rem(self.lon + 16 + shift + 8 * self.top, 16))

    def lower(self, shift):
        return (self.south, lax.rem(self.lon + 16 + shift + 8 * self.bottom, 16))

    def beside(self, shift):
        return (self.lat, lax.rem(self.lon + 16 + shift, 16))

    def everyone(self):
        return [self.upper(s) for s in (0, -1, 1)] + [self.lower(s) for s in (0, -1, 1)] + [self.beside(-1), self.beside(1)]

    def send(self, ext, send, recv):
        own = slice(reach, reach + cols)
        first, last = slice(reach, 2 * reach), slice(cols, cols + reach)
        left, right = slice(0, reach), slice(reach + cols, wide)
        copies = []
        copies.append(remote(ext.at[1 : rows + 1, first], ext.at[1 : rows + 1, right], send.at[6], recv.at[6], self.beside(-1)))
        copies.append(remote(ext.at[1 : rows + 1, last], ext.at[1 : rows + 1, left], send.at[7], recv.at[7], self.beside(1)))
        for number, (side, target, row) in enumerate(((self.side_n, self.upper, 1), (self.side_s, self.lower, rows))):
            to = side * (rows + 1)
            plan = ((own, own, 0), (first, right, -1), (last, left, 1))
            for part, (src, dst, shift) in enumerate(plan):
                copies.append(
                    remote(
                        ext.at[row, src], ext.at[to, dst], send.at[number * 3 + part], recv.at[side * 3 + part], target(shift)
                    )
                )
        for copy in copies:
            copy.start()
        return copies

    def wait_columns(self, ext, send, recv):
        me = self.beside(1)
        for number, first in ((6, reach + cols), (7, 0)):
            here = ext.at[1 : rows + 1, first : first + reach]
            remote(here, here, send.at[0], recv.at[number], me).wait_recv()

    def wait_rows(self, ext, send, recv):
        own = slice(reach, reach + cols)
        left, right = slice(0, reach), slice(reach + cols, wide)
        me = self.beside(1)
        for side in range(2):
            for part, where in enumerate((own, right, left)):
                here = ext.at[side * (rows + 1), where]
                remote(here, here, send.at[0], recv.at[side * 3 + part], me).wait_recv()


def toeplitz(row):
    spread = jnp.broadcast_to(row, (cols, wide))
    return pltpu.roll(spread, 0, 1, stride=1, stride_axis=0).astype(bf16)


def step_kernel(
    scale,
    field_in, taps_in, mix_in, up_in, down_in, cot_in,
    block_rows, field_rows, total,
    ext, gext, band, adjoint, tapx, revx, feats, cot, hidden, act_grad, act, pre_grad, mix, up, down,
    grads,
    load_sem, halo_send, halo_recv, grad_send, grad_recv, tap_send, tap_recv,
    *rest,
):
    place = Place()
    halo = Halo(place)
    own = slice(reach, reach + cols)

    loads = [
        pltpu.make_async_copy(taps_in, tapx.at[:, 1 : rows + 1], load_sem.at[0]),
        pltpu.make_async_copy(field_in, ext.at[1 : rows + 1, own], load_sem.at[1]),
        pltpu.make_async_copy(cot_in, cot, load_sem.at[2]),
        pltpu.make_async_copy(down_in, down, load_sem.at[3]),
        pltpu.make_async_copy(mix_in, mix, load_sem.at[4]),
        pltpu.make_async_copy(up_in, up, load_sem.at[5]),
    ]
    for load in loads:
        load.start()
    devices = place.everyone() + halo.everyone()
    barrier = pltpu.get_barrier_semaphore()
    for device in devices:
        pl.semaphore_signal(barrier, inc=1, device_id=device, device_id_type=MESH)

    loads[0].wait()

    def build(r, carry):
        for k in range(basis):
            for d in range(3):
                band[r, k * cols : (k + 1) * cols, d * wide : (d + 1) * wide] = toeplitz(
                    tapx[k, r + 1, d : d + 1, :]
                )
        return carry

    lax.fori_loop(0, rows, build, 0)
    loads[1].wait()
    pl.semaphore_wait(barrier, len(devices))
    sent = halo.send(ext, halo_send, halo_recv)
    tap_copies = [
        remote(tapx.at[:, 1], tapx.at[:, halo.side_n * (rows + 1)], tap_send.at[0], tap_recv.at[halo.side_n], halo.upper(0)),
        remote(tapx.at[:, rows], tapx.at[:, halo.side_s * (rows + 1)], tap_send.at[1], tap_recv.at[halo.side_s], halo.lower(0)),
    ]
    for copy in tap_copies:
        copy.start()
    sent += tap_copies

    loads[2].wait()
    loads[3].wait()

    def early(i, carry):
        at = pl.ds(multiple(i * chunk, 16), chunk)
        grad = cot[pl.ds(i * chunk_rows, chunk_rows)].reshape(chunk, lanes)
        act_grad[at, :] = mm_nt(grad, down[...])
        return carry

    lax.fori_loop(0, chunks, early, 0)

    row_at = lax.broadcasted_iota(jnp.int32, (wide, wide), 0)
    mirror = (row_at + lax.broadcasted_iota(jnp.int32, (wide, wide), 1) == taps - 1).astype(f32).astype(bf16)
    straight = tapx[:, 1 : rows + 1].reshape(basis * rows * 8, wide).astype(bf16)
    revx[:, 1 : rows + 1] = mm(straight, mirror).reshape(basis, rows, 8, wide)

    def build_back(r, carry):
        for k in range(basis):
            for s in range(3):
                adjoint[r, k * cols : (k + 1) * cols, s * wide : (s + 1) * wide] = toeplitz(revx[k, r + s, 2 - s : 3 - s, :])
        return carry

    lax.fori_loop(1, rows - 1, build_back, 0)

    loads[4].wait()
    loads[5].wait()
    halo.wait_columns(ext, halo_send, halo_recv)

    def features(r, carry):
        window = ext[pl.ds(r, 3)].reshape(depth, lanes)
        made = mm(band[r], window).astype(bf16)
        at = pl.ds(multiple(r * cols, 16), cols)
        for k in range(basis):
            feats[k, at, :] = made[k * cols : (k + 1) * cols]
        return carry

    lax.fori_loop(1, rows - 1, features, 0)
    halo.wait_rows(ext, halo_send, halo_recv)
    features(0, 0)
    features(rows - 1, 0)

    def pointwise(i, carry):
        at = pl.ds(multiple(i * chunk, 16), chunk)
        total = ext[pl.ds(1 + i * chunk_rows, chunk_rows), own].reshape(chunk, lanes).astype(f32)
        for k in range(basis):
            total = total + mm(feats[k, at, :], mix[k])
        inner = total.astype(bf16)
        hidden[at, :] = inner
        for block in range(hidden_units // 256):
            f = slice(block * 256, (block + 1) * 256)
            value = mm(inner, up[:, f])
            cdf = 0.5 * (1.0 + lax.erf(value * inv_root_two))
            act[at, f] = (value * cdf).astype(bf16)
            slope = cdf + value * jnp.exp(-0.5 * value * value) * inv_root_tau
            pre_grad[at, f] = (act_grad[at, f] * slope).astype(bf16)
        made = (inner.astype(f32) + mm(act[at, :], down[...])).astype(bf16)
        block_rows[pl.ds(i * chunk_rows, chunk_rows)] = made.reshape(chunk_rows, cols, lanes)
        grad = cot[pl.ds(i * chunk_rows, chunk_rows)].reshape(chunk, lanes).astype(f32)
        grad = (grad + mm_nt(pre_grad[at, :], up[...])).astype(bf16)
        gext[pl.ds(1 + i * chunk_rows, chunk_rows), own] = grad.reshape(chunk_rows, cols, lanes)
        return carry

    lax.fori_loop(0, chunks, pointwise, 0)
    sent += halo.send(gext, grad_send, grad_recv)

    def flat(ref):
        return ref[...].reshape(points, lanes)

    sums = [
        Reduction(place, start, count, grads, total, rest[8 * n : 8 * n + 8], rest[32 + 2 * n], rest[33 + 2 * n], scale)
        for n, (start, count) in enumerate(stacks)
    ]
    sum_up, sum_down, sum_mix, sum_rest = sums

    def weight_down(i, carry):
        part = pl.ds(multiple(i * 256, 256), 256)
        grads[pl.ds(multiple(1024 + i * 256, 256), 256), :] = mm_tn(act[:, part], flat(cot)).astype(bf16)
        return carry

    lax.fori_loop(0, 4, weight_down, 0)
    sum_down.start_pair()

    def weight_up(i, carry):
        part = pl.ds(multiple(i * 256, 256), 256)
        left = hidden[:, part]
        for side in range(2):
            grads[pl.ds(multiple(side * 512 + i * 256, 256), 256), :] = mm_tn(
                left, pre_grad[:, side * 512 : side * 512 + 512]
            ).astype(bf16)
        return carry

    lax.fori_loop(0, 2, weight_up, 0)
    sum_up.start_pair()
    sum_down.pair_then_first()

    def weight_mix(i, carry):
        k, half = lax.div(i, 2), lax.rem(i, 2)
        part = pl.ds(multiple(half * 256, 256), 256)
        grad = gext[1 : rows + 1, own].reshape(points, lanes)
        grads[pl.ds(multiple(2048 + i * 256, 256), 256), :] = mm_tn(feats[k, :, part], grad).astype(bf16)
        return carry

    lax.fori_loop(0, 4, weight_mix, 0)
    sum_mix.start_pair()
    sum_up.pair_then_first()
    lax.fori_loop(4, 6, weight_mix, 0)
    sum_rest.start_pair()
    sum_mix.pair_then_first()

    for side in range(2):
        here = tapx.at[:, side * (rows + 1)]
        remote(here, here, tap_send.at[0], tap_recv.at[side], halo.beside(1)).wait_recv()
    for r, pole in ((0, halo.top), (rows - 1, halo.bottom)):
        slot = 0 if r == 0 else rows + 1
        straight = tapx[:, slot].reshape(basis * 8, wide).astype(bf16)
        revx[:, slot] = mm(straight, mirror).reshape(basis, 8, wide)
        for k in range(basis):
            for s in range(3):
                row = revx[k, r + s, 2 - s : 3 - s, :]
                if r + s == slot:
                    row = jnp.where(pole == 1, revx[k, r + s, s : s + 1, :], row)
                adjoint[r, k * cols : (k + 1) * cols, s * wide : (s + 1) * wide] = toeplitz(row)

    def pull(r, carry):
        window = gext[pl.ds(r, 3)].reshape(depth, lanes)
        made = mm(adjoint[r], window).astype(bf16)
        at = pl.ds(multiple(r * cols, 16), cols)
        for k in range(basis):
            feats[k, at, :] = made[k * cols : (k + 1) * cols]
        return carry

    halo.wait_columns(gext, grad_send, grad_recv)
    lax.fori_loop(1, rows // 2, pull, 0)
    sum_rest.pair_then_first()
    lax.fori_loop(rows // 2, rows - 1, pull, 0)
    halo.wait_rows(gext, grad_send, grad_recv)
    pull(0, 0)
    pull(rows - 1, 0)
    sum_down.first_then_second()

    def last(i, carry):
        at = pl.ds(multiple(i * chunk, 16), chunk)
        made = gext[pl.ds(1 + i * chunk_rows, chunk_rows), own].reshape(chunk, lanes).astype(f32)
        for k in range(basis):
            made = made + mm_nt(feats[k, at, :], mix[k])
        field_rows[pl.ds(i * chunk_rows, chunk_rows)] = made.astype(bf16).reshape(chunk_rows, cols, lanes)
        return carry

    lax.fori_loop(0, 2, last, 0)
    sum_up.first_then_second()
    sum_down.second_then_z()
    lax.fori_loop(2, chunks, last, 0)
    stages = ("first_then_second", "second_then_z", "z_then_back", "back_second", "back_first", "back_pair", "finish")
    order = (sum_down, sum_up, sum_mix, sum_rest)
    done = {sum_down: 2, sum_up: 1, sum_mix: 0, sum_rest: 0}
    for wave in range(2, len(stages) + len(order)):
        for number in range(len(order)):
            item, stage = order[number], wave - number
            if done[item] <= stage < len(stages):
                getattr(item, stages[stage])()
    for copy in sent:
        copy.wait_send()


def local(field_in, kernel_taps, row_reach, mix_weight, up_weight, down_weight, cotangent):
    offsets = jnp.arange(wide, dtype=jnp.int32) - reach
    mask = jnp.abs(offsets)[None, :] <= row_reach[:, None]
    tap_rows = jnp.pad(kernel_taps, ((0, 0), (0, 0), (0, 5), (0, wide - taps))).astype(f32)
    tap_rows = jnp.where(mask[None, :, None, :], tap_rows, 0.0)
    total_points = points * lax.axis_size("lat") * lax.axis_size("lon")
    scale = 1.0 / math.sqrt(total_points)
    anywhere = pl.BlockSpec(memory_space=pl.ANY)
    v = pltpu.VMEM
    dma = pltpu.SemaphoreType.DMA
    resident = pl.BlockSpec(memory_space=pltpu.VMEM)
    shape = jax.ShapeDtypeStruct
    made = pl.pallas_call(
        lambda *refs: step_kernel(scale, *refs),
        out_shape=(
            shape(field_in.shape, bf16), shape(field_in.shape, bf16), shape((3584, lanes), bf16),
        ),
        in_specs=[anywhere] * 6,
        out_specs=(resident,) * 3,
        scratch_shapes=[
            v((rows + 2, wide, lanes), bf16),
            v((rows + 2, wide, lanes), bf16),
            v((rows, span, depth), bf16),
            v((rows, span, depth), bf16),
            v((basis, rows + 2, 8, wide), f32),
            v((basis, rows + 2, 8, wide), f32),
            v((basis, points, lanes), bf16),
            v((rows, cols, lanes), bf16),
            v((points, lanes), bf16),
            v((points, hidden_units), f32),
            v((points, hidden_units), bf16),
            v((points, hidden_units), bf16),
            v((basis, lanes, lanes), bf16),
            v((lanes, hidden_units), bf16),
            v((hidden_units, lanes), bf16),
            v((3584, lanes), bf16),
            dma((6,)), dma((8,)), dma((8,)), dma((8,)), dma((8,)), dma((2,)), dma((2,)),
        ]
        + [part for start, count in stacks for part in Reduction.scratch(count)]
        + [dma((copies_each,)) for _ in range(2 * len(stacks))],
        compiler_params=pltpu.CompilerParams(
            collective_id=0, has_side_effects=True, vmem_limit_bytes=vmem_room
        ),
        name="disco_step",
    )(*[pltpu.with_memory_space_constraint(x, pltpu.HBM) for x in (field_in, tap_rows, mix_weight, up_weight, down_weight, cotangent)])
    return store_all(*[pltpu.with_memory_space_constraint(x, pltpu.VMEM) for x in made])


def store_kernel(block_rows, field_rows, total, block_out, field_out, mix_out, up_out, down_out, sem):
    stores = [
        pltpu.make_async_copy(block_rows, block_out, sem.at[0]),
        pltpu.make_async_copy(field_rows, field_out, sem.at[1]),
        pltpu.make_async_copy(total.at[0:512], up_out.at[:, 0:512], sem.at[2]),
        pltpu.make_async_copy(total.at[512:1024], up_out.at[:, 512:1024], sem.at[3]),
        pltpu.make_async_copy(total.at[1024:2048], down_out, sem.at[4]),
    ]
    for k in range(basis):
        stores.append(pltpu.make_async_copy(total.at[2048 + k * 512 : 2560 + k * 512], mix_out.at[k], sem.at[5 + k]))
    for store in stores:
        store.start()
    for store in stores:
        store.wait()


def store_all(block_rows, field_rows, total):
    shape = jax.ShapeDtypeStruct
    return pl.pallas_call(
        store_kernel,
        out_shape=(
            shape(block_rows.shape, bf16), shape(field_rows.shape, bf16), shape((basis, lanes, lanes), bf16),
            shape((lanes, hidden_units), bf16), shape((hidden_units, lanes), bf16),
        ),
        in_specs=[pl.BlockSpec(memory_space=pltpu.VMEM)] * 3,
        out_specs=(pl.BlockSpec(memory_space=pltpu.HBM),) * 5,
        scratch_shapes=[pltpu.SemaphoreType.DMA((8,))],
        compiler_params=pltpu.CompilerParams(vmem_limit_bytes=1024 * 1024),
        name="store_all",
    )(block_rows, field_rows, total)


def solution(mesh):
    placed = (
        P("lat", "lon", None),
        P(None, "lat", None, None),
        P("lat"),
        P(),
        P(),
        P(),
        P("lat", "lon", None),
    )
    return jax.shard_map(
        local,
        mesh=mesh,
        in_specs=placed,
        out_specs=(P("lat", "lon", None), P("lat", "lon", None), P(), P(), P()),
        check_vma=False,
    )
```

```python
import math

import jax
import jax.numpy as jnp
from jax import lax
from jax.experimental import pallas as pl
from jax.experimental.pallas import tpu as pltpu
from jax.sharding import PartitionSpec as P

inv_root_two = 0.7071067811865476
inv_root_tau = 0.3989422804014327

MESH = pl.DeviceIdType.MESH
ring_xy = 4
ring_z = 8
lanes = 512


def multiple(value, of):
    return pl.multiple_of(value, of)


def remote(src, dst, send_sem, recv_sem, device):
    return pltpu.make_async_remote_copy(
        src_ref=src, dst_ref=dst, send_sem=send_sem, recv_sem=recv_sem, device_id=device, device_id_type=MESH
    )


class Place:
    def __init__(self):
        self.lat = lax.axis_index("lat")
        self.lon = lax.axis_index("lon")
        self.z = lax.rem(self.lat, ring_z)
        self.core = lax.rem(self.lon, 2)
        self.y = lax.div(self.lon, 4)
        self.x = lax.rem(lax.div(self.lon, 2), 2) * 2 + lax.div(self.lat, ring_z)
        self.first = self.x * (1 - self.core) + self.y * self.core
        self.second = self.y * (1 - self.core) + self.x * self.core

    def device(self, x, y, z, core):
        return (lax.rem(x, 2) * ring_z + z, y * 4 + lax.div(x, 2) * 2 + core)

    def partner(self):
        return self.device(self.x, self.y, self.z, 1 - self.core)

    def along_x(self, step):
        return self.device(lax.rem(self.x + step, ring_xy), self.y, self.z, self.core)

    def along_y(self, step):
        return self.device(self.x, lax.rem(self.y + step, ring_xy), self.z, self.core)

    def along_z(self, step):
        return self.device(self.x, self.y, lax.rem(self.z + step, ring_z), self.core)

    def along_first(self, step):
        x = lax.rem(self.x + step * (1 - self.core), ring_xy)
        y = lax.rem(self.y + step * self.core, ring_xy)
        return self.device(x, y, self.z, self.core)

    def along_second(self, step):
        x = lax.rem(self.x + step * self.core, ring_xy)
        y = lax.rem(self.y + step * (1 - self.core), ring_xy)
        return self.device(x, y, self.z, self.core)

    def everyone(self):
        found = [self.partner()]
        found += [self.along_x(s) for s in range(1, ring_xy)]
        found += [self.along_y(s) for s in range(1, ring_xy)]
        found += [self.along_z(s) for s in range(1, ring_z)]
        return found


def add_rows(dst, dst_at, sources, count, chunk):
    def body(i, carry):
        total = None
        for ref, at in sources:
            term = ref[pl.ds(multiple(at + i * chunk, 16), chunk), :].astype(jnp.float32)
            total = term if total is None else total + term
        dst[pl.ds(multiple(dst_at + i * chunk, 16), chunk), :] = total.astype(dst.dtype)
        return carry

    lax.fori_loop(0, count // chunk, body, 0)


wire_steps = (2, 1, 3)
z_steps = (4, 3, 5, 2, 6, 1, 7)


class Reduction:
    def __init__(self, place, start, rows, grad, out, parts, send, recv, scale):
        self.p = place
        self.half, self.quarter, self.piece = rows // 2, rows // 8, rows // 32
        self.grad, self.out, self.scale = grad.at[start : start + rows], out.at[start : start + rows], scale
        self.r0, self.s0, self.r1, self.s1, self.r2, self.s2, self.r3, self.zbuf = parts
        self.send, self.recv = send, recv
        self.used = 0
        self.sent = []

    @staticmethod
    def scratch(rows):
        half, quarter, piece = rows // 2, rows // 8, rows // 32
        shapes = [
            (half, lanes), (half, lanes), (3, quarter, lanes), (quarter, lanes),
            (3, piece, lanes), (32, lanes), (7, 16, 128), (32, lanes),
        ]
        return [pltpu.VMEM(s, jnp.bfloat16) for s in shapes]

    def go(self, src, dst, device):
        copy = remote(src, dst, self.send.at[self.used], self.recv.at[self.used], device)
        self.used += 1
        copy.start()
        self.sent.append(copy)
        return copy

    def start_pair(self):
        p = self.p
        other = multiple((1 - p.core) * self.half, 16)
        self.flight = [self.go(self.grad.at[pl.ds(other, self.half), :], self.r0, p.partner())]

    def arrived(self):
        for copy in self.flight:
            copy.wait_recv()
        self.flight = []

    def block(self, ref, index, part):
        half = self.quarter // 2
        return ref.at[pl.ds(multiple(index * self.quarter + part * half, 16), half), :]

    def pair_then_first(self):
        p = self.p
        self.arrived()
        half = self.quarter // 2
        place = [lax.rem(p.first + step, ring_xy) for step in range(ring_xy)]

        def join(step):
            at = place[step] * self.quarter
            add_rows(self.s0, at, [(self.grad, p.core * self.half + at), (self.r0, at)], self.quarter, 64)

        top, low = self.r1.at[2, 0:half], self.r1.at[2, half : 2 * half]
        join(2)
        self.relayed = [
            self.go(self.block(self.s0, place[2], 0), top, p.along_first(1)),
            self.go(self.block(self.s0, place[2], 1), low, p.along_first(3)),
        ]
        join(1)
        self.flight = [self.go(self.block(self.s0, place[1], 1), self.r1.at[0, half : 2 * half], p.along_first(1))]
        join(3)
        self.flight.append(self.go(self.block(self.s0, place[3], 0), self.r1.at[1, 0:half], p.along_first(3)))
        join(0)

    def first_relay(self):
        p = self.p
        half = self.quarter // 2
        for copy, step, part in ((self.relayed[0], 1, 0), (self.relayed[1], 3, 1)):
            copy.wait_recv()
            index = lax.rem(p.first + step, ring_xy)
            at = index * self.quarter + part * half
            add_rows(self.s0, at, [(self.s0, at), (self.r1.at[2], part * half)], half, half)
            land = self.r1.at[0 if step == 1 else 1, part * half : part * half + half]
            self.flight.append(self.go(self.block(self.s0, index, part), land, p.along_first(step)))

    def first_then_second(self):
        p = self.p
        self.arrived()
        flight = []
        own = p.first * self.quarter
        for step in (2, 1, 3, 0):
            at = lax.rem(p.second + step, ring_xy) * self.piece
            sources = [(self.s0, own + at)] + [(self.r1.at[i], at) for i in range(2)]
            add_rows(self.s1, at, sources, self.piece, 16)
            if step:
                src = self.s1.at[pl.ds(multiple(at, 16), self.piece), :]
                flight.append(self.go(src, self.r2.at[step - 1], p.along_second(step)))
        self.flight = flight

    def spot(self, ref, index):
        row = multiple(lax.div(index, 4) * 16, 16)
        lane = multiple(lax.rem(index, 4) * 128, 128)
        return ref.at[pl.ds(row, 16), pl.ds(lane, 128)]

    def second_then_z(self):
        p = self.p
        self.arrived()
        sources = [(self.s1, p.second * self.piece)] + [(self.r2.at[i], 0) for i in range(3)]
        add_rows(self.s2, 0, sources, self.piece, 16)
        if self.piece < 32:
            self.s2[self.piece :, :] = jnp.zeros((32 - self.piece, lanes), jnp.bfloat16)
        flight = []
        for step in z_steps:
            src = self.spot(self.s2, lax.rem(p.z + step, ring_z))
            flight.append(self.go(src, self.r3.at[step - 1], p.along_z(step)))
        self.flight = flight

    def z_then_back(self):
        p = self.p
        self.arrived()
        total = self.spot(self.s2, p.z)[...].astype(jnp.float32)
        for i in range(7):
            total = total + self.r3[i].astype(jnp.float32)
        mine = self.spot(self.zbuf, p.z)
        mine[...] = (total * self.scale).astype(jnp.bfloat16)
        self.flight = [self.go(mine, mine, p.along_z(step)) for step in z_steps]

    def back_second(self):
        p = self.p
        self.arrived()
        at = p.core * self.half + p.first * self.quarter + p.second * self.piece
        mine = self.out.at[pl.ds(multiple(at, 16), self.piece), :]
        mine[...] = self.zbuf[: self.piece, :]
        self.flight = [self.go(mine, mine, p.along_second(step)) for step in wire_steps]

    def back_first(self):
        p = self.p
        self.arrived()
        mine = self.out.at[pl.ds(multiple(p.core * self.half, 16), self.half), :]
        parts = [self.block(mine, p.first, part) for part in range(2)]
        self.relayed = [self.go(parts[0], parts[0], p.along_first(1)), self.go(parts[1], parts[1], p.along_first(3))]
        self.flight = [self.go(parts[1], parts[1], p.along_first(1)), self.go(parts[0], parts[0], p.along_first(3))]

    def back_relay(self):
        p = self.p
        mine = self.out.at[pl.ds(multiple(p.core * self.half, 16), self.half), :]
        for copy, step, part in ((self.relayed[0], 1, 0), (self.relayed[1], 3, 1)):
            copy.wait_recv()
            came = self.block(mine, lax.rem(p.first + ring_xy - step, ring_xy), part)
            self.flight.append(self.go(came, came, p.along_first(step)))

    def back_pair(self):
        p = self.p
        self.arrived()
        mine = self.out.at[pl.ds(multiple(p.core * self.half, 16), self.half), :]
        self.flight = [self.go(mine, mine, p.partner())]

    def finish(self):
        self.arrived()
        for copy in self.sent:
            copy.wait_send()


copies_each = 34
stacks = ((0, 1024), (1024, 1024), (2048, 1024), (3072, 512))


rows = 10
cols = 96
reach = 16
vmem_room = 48 * 1024 * 1024
wide = cols + 2 * reach
taps = 2 * reach + 1
basis = 3
points = rows * cols
hidden_units = 1024
chunk_rows = 2
chunk = chunk_rows * cols
chunks = rows // chunk_rows
span = basis * cols
depth = 3 * wide
f32 = jnp.float32
bf16 = jnp.bfloat16


def mm(a, b):
    return jnp.dot(a, b, preferred_element_type=f32)


def mm_nt(a, b):
    return lax.dot_general(a, b, (((1,), (1,)), ((), ())), preferred_element_type=f32)


def mm_tn(a, b):
    return lax.dot_general(a, b, (((0,), (0,)), ((), ())), preferred_element_type=f32)


class Halo:
    def __init__(self, place):
        lat, lon = place.lat, place.lon
        top = (lat == 0).astype(jnp.int32)
        bottom = (lat == 15).astype(jnp.int32)
        self.top, self.bottom = top, bottom
        self.lat, self.lon = lat, lon
        self.north = lat - 1 + top
        self.south = lat + 1 - bottom
        self.side_n = 1 - top
        self.side_s = bottom

    def upper(self, shift):
        return (self.north, lax.rem(self.lon + 16 + shift + 8 * self.top, 16))

    def lower(self, shift):
        return (self.south, lax.rem(self.lon + 16 + shift + 8 * self.bottom, 16))

    def beside(self, shift):
        return (self.lat, lax.rem(self.lon + 16 + shift, 16))

    def everyone(self):
        return [self.upper(s) for s in (0, -1, 1)] + [self.lower(s) for s in (0, -1, 1)] + [self.beside(-1), self.beside(1)]

    def send(self, ext, send, recv):
        own = slice(reach, reach + cols)
        first, last = slice(reach, 2 * reach), slice(cols, cols + reach)
        left, right = slice(0, reach), slice(reach + cols, wide)
        copies = []
        copies.append(remote(ext.at[1 : rows + 1, first], ext.at[1 : rows + 1, right], send.at[6], recv.at[6], self.beside(-1)))
        copies.append(remote(ext.at[1 : rows + 1, last], ext.at[1 : rows + 1, left], send.at[7], recv.at[7], self.beside(1)))
        for number, (side, target, row) in enumerate(((self.side_n, self.upper, 1), (self.side_s, self.lower, rows))):
            to = side * (rows + 1)
            plan = ((own, own, 0), (first, right, -1), (last, left, 1))
            for part, (src, dst, shift) in enumerate(plan):
                copies.append(
                    remote(
                        ext.at[row, src], ext.at[to, dst], send.at[number * 3 + part], recv.at[side * 3 + part], target(shift)
                    )
                )
        for copy in copies:
            copy.start()
        return copies

    def wait_columns(self, ext, send, recv):
        me = self.beside(1)
        for number, first in ((6, reach + cols), (7, 0)):
            here = ext.at[1 : rows + 1, first : first + reach]
            remote(here, here, send.at[0], recv.at[number], me).wait_recv()

    def wait_rows(self, ext, send, recv):
        own = slice(reach, reach + cols)
        left, right = slice(0, reach), slice(reach + cols, wide)
        me = self.beside(1)
        for side in range(2):
            for part, where in enumerate((own, right, left)):
                here = ext.at[side * (rows + 1), where]
                remote(here, here, send.at[0], recv.at[side * 3 + part], me).wait_recv()


def toeplitz(row):
    spread = jnp.broadcast_to(row, (cols, wide))
    return pltpu.roll(spread, 0, 1, stride=1, stride_axis=0).astype(bf16)


def step_kernel(
    scale,
    field_in, taps_in, reach_in, mix_in, up_in, down_in, cot_in,
    block_rows, field_rows, total,
    ext, gext, band, adjoint, traw, far, tapx, revx, feats, cot, hidden, act_grad, act, pre_grad, mix, up, down,
    grads,
    load_sem, halo_send, halo_recv, grad_send, grad_recv, tap_send, tap_recv,
    *rest,
):
    place = Place()
    halo = Halo(place)
    own = slice(reach, reach + cols)

    loads = [
        pltpu.make_async_copy(taps_in, traw, load_sem.at[0]),
        pltpu.make_async_copy(reach_in, far, load_sem.at[6]),
        pltpu.make_async_copy(field_in, ext.at[1 : rows + 1, own], load_sem.at[1]),
        pltpu.make_async_copy(cot_in, cot, load_sem.at[2]),
        pltpu.make_async_copy(down_in, down, load_sem.at[3]),
        pltpu.make_async_copy(mix_in, mix, load_sem.at[4]),
        pltpu.make_async_copy(up_in, up, load_sem.at[5]),
    ]
    for load in loads:
        load.start()
    devices = place.everyone() + halo.everyone()
    barrier = pltpu.get_barrier_semaphore()
    for device in devices:
        pl.semaphore_signal(barrier, inc=1, device_id=device, device_id_type=MESH)

    loads[0].wait()

    loads[1].wait()
    tap_at = lax.broadcasted_iota(jnp.int32, (taps, 2 * wide), 0)
    spot_at = lax.broadcasted_iota(jnp.int32, (taps, 2 * wide), 1)
    select = ((spot_at == tap_at) | (spot_at == wide + taps - 1 - tap_at)).astype(f32).astype(bf16)
    away = jnp.abs(lax.broadcasted_iota(jnp.int32, (3, taps), 1) - reach)
    revx[:, 1 : rows + 1] = jnp.zeros((basis, rows, 8, wide), f32)

    def build(r, carry):
        for k in range(basis):
            kept = jnp.where(away <= far[r], traw[k, r].astype(f32), 0.0).astype(bf16)
            both = mm(kept, select)
            tapx[k, r + 1, 0:3, :] = both[:, :wide]
            revx[k, r + 1, 0:3, :] = both[:, wide:]
        for k in range(basis):
            for d in range(3):
                band[r, k * cols : (k + 1) * cols, d * wide : (d + 1) * wide] = toeplitz(
                    tapx[k, r + 1, d : d + 1, :]
                )
        return carry

    lax.fori_loop(0, rows, build, 0)
    loads[2].wait()
    pl.semaphore_wait(barrier, len(devices))
    sent = halo.send(ext, halo_send, halo_recv)
    tap_copies = [
        remote(revx.at[:, 1], revx.at[:, halo.side_n * (rows + 1)], tap_send.at[0], tap_recv.at[halo.side_n], halo.upper(0)),
        remote(revx.at[:, rows], revx.at[:, halo.side_s * (rows + 1)], tap_send.at[1], tap_recv.at[halo.side_s], halo.lower(0)),
    ]
    for copy in tap_copies:
        copy.start()
    sent += tap_copies

    loads[3].wait()
    loads[4].wait()

    def early(i, carry):
        at = pl.ds(multiple(i * chunk, 16), chunk)
        grad = cot[pl.ds(i * chunk_rows, chunk_rows)].reshape(chunk, lanes)
        act_grad[at, :] = mm_nt(grad, down[...])
        return carry

    lax.fori_loop(0, chunks, early, 0)

    def build_back(r, carry):
        for k in range(basis):
            for s in range(3):
                adjoint[r, k * cols : (k + 1) * cols, s * wide : (s + 1) * wide] = toeplitz(revx[k, r + s, 2 - s : 3 - s, :])
        return carry

    lax.fori_loop(1, rows - 1, build_back, 0)

    loads[5].wait()
    loads[6].wait()
    halo.wait_columns(ext, halo_send, halo_recv)

    def features(r, carry):
        window = ext[pl.ds(r, 3)].reshape(depth, lanes)
        made = mm(band[r], window).astype(bf16)
        at = pl.ds(multiple(r * cols, 16), cols)
        for k in range(basis):
            feats[k, at, :] = made[k * cols : (k + 1) * cols]
        return carry

    lax.fori_loop(1, rows - 1, features, 0)
    halo.wait_rows(ext, halo_send, halo_recv)
    features(0, 0)
    features(rows - 1, 0)

    def pointwise(i, carry):
        at = pl.ds(multiple(i * chunk, 16), chunk)
        total = ext[pl.ds(1 + i * chunk_rows, chunk_rows), own].reshape(chunk, lanes).astype(f32)
        for k in range(basis):
            total = total + mm(feats[k, at, :], mix[k])
        inner = total.astype(bf16)
        hidden[at, :] = inner
        for block in range(hidden_units // 256):
            f = slice(block * 256, (block + 1) * 256)
            value = mm(inner, up[:, f])
            cdf = 0.5 * (1.0 + lax.erf(value * inv_root_two))
            act[at, f] = (value * cdf).astype(bf16)
            slope = cdf + value * jnp.exp(-0.5 * value * value) * inv_root_tau
            pre_grad[at, f] = (act_grad[at, f] * slope).astype(bf16)
        made = (inner.astype(f32) + mm(act[at, :], down[...])).astype(bf16)
        block_rows[pl.ds(i * chunk_rows, chunk_rows)] = made.reshape(chunk_rows, cols, lanes)
        grad = cot[pl.ds(i * chunk_rows, chunk_rows)].reshape(chunk, lanes).astype(f32)
        grad = (grad + mm_nt(pre_grad[at, :], up[...])).astype(bf16)
        gext[pl.ds(1 + i * chunk_rows, chunk_rows), own] = grad.reshape(chunk_rows, cols, lanes)
        return carry

    lax.fori_loop(0, chunks, pointwise, 0)
    sent += halo.send(gext, grad_send, grad_recv)

    def flat(ref):
        return ref[...].reshape(points, lanes)

    sums = [
        Reduction(place, start, count, grads, total, rest[8 * n : 8 * n + 8], rest[32 + 2 * n], rest[33 + 2 * n], scale)
        for n, (start, count) in enumerate(stacks)
    ]
    sum_up, sum_down, sum_mix, sum_rest = sums

    def weight_down(i, carry):
        part = pl.ds(multiple(i * 256, 256), 256)
        grads[pl.ds(multiple(1024 + i * 256, 256), 256), :] = mm_tn(act[:, part], flat(cot)).astype(bf16)
        return carry

    lax.fori_loop(0, 4, weight_down, 0)
    sum_down.start_pair()

    def weight_up(i, carry):
        part = pl.ds(multiple(i * 256, 256), 256)
        left = hidden[:, part]
        for side in range(2):
            grads[pl.ds(multiple(side * 512 + i * 256, 256), 256), :] = mm_tn(
                left, pre_grad[:, side * 512 : side * 512 + 512]
            ).astype(bf16)
        return carry

    lax.fori_loop(0, 2, weight_up, 0)
    sum_up.start_pair()
    sum_down.pair_then_first()

    def weight_mix(i, carry):
        k, half = lax.div(i, 2), lax.rem(i, 2)
        part = pl.ds(multiple(half * 256, 256), 256)
        grad = gext[1 : rows + 1, own].reshape(points, lanes)
        grads[pl.ds(multiple(2048 + i * 256, 256), 256), :] = mm_tn(feats[k, :, part], grad).astype(bf16)
        return carry

    lax.fori_loop(0, 4, weight_mix, 0)
    sum_mix.start_pair()
    sum_up.pair_then_first()
    sum_down.first_relay()
    lax.fori_loop(4, 6, weight_mix, 0)
    sum_rest.start_pair()
    sum_mix.pair_then_first()
    sum_up.first_relay()

    for side in range(2):
        here = revx.at[:, side * (rows + 1)]
        remote(here, here, tap_send.at[0], tap_recv.at[side], halo.beside(1)).wait_recv()
    for r, pole in ((0, halo.top), (rows - 1, halo.bottom)):
        slot = 0 if r == 0 else rows + 1
        for k in range(basis):
            for s in range(3):
                row = revx[k, r + s, 2 - s : 3 - s, :]
                if r + s == slot:
                    row = jnp.where(pole == 1, revx[k, r + s, s : s + 1, :], row)
                adjoint[r, k * cols : (k + 1) * cols, s * wide : (s + 1) * wide] = toeplitz(row)

    def pull(r, carry):
        window = gext[pl.ds(r, 3)].reshape(depth, lanes)
        made = mm(adjoint[r], window).astype(bf16)
        at = pl.ds(multiple(r * cols, 16), cols)
        for k in range(basis):
            feats[k, at, :] = made[k * cols : (k + 1) * cols]
        return carry

    halo.wait_columns(gext, grad_send, grad_recv)
    lax.fori_loop(1, rows // 2, pull, 0)
    sum_rest.pair_then_first()
    sum_mix.first_relay()
    lax.fori_loop(rows // 2, rows - 1, pull, 0)
    halo.wait_rows(gext, grad_send, grad_recv)
    pull(0, 0)
    pull(rows - 1, 0)
    sum_rest.first_relay()

    def last(i, carry):
        at = pl.ds(multiple(i * chunk, 16), chunk)
        made = gext[pl.ds(1 + i * chunk_rows, chunk_rows), own].reshape(chunk, lanes).astype(f32)
        for k in range(basis):
            made = made + mm_nt(feats[k, at, :], mix[k])
        field_rows[pl.ds(i * chunk_rows, chunk_rows)] = made.astype(bf16).reshape(chunk_rows, cols, lanes)
        return carry

    lax.fori_loop(0, 2, last, 0)
    sum_down.first_then_second()
    lax.fori_loop(2, chunks, last, 0)
    order = (sum_down, sum_up, sum_mix, sum_rest)
    for item in order[1:]:
        item.first_then_second()
    for stage in ("second_then_z", "z_then_back", "back_second", "back_first", "back_relay", "back_pair", "finish"):
        for item in order:
            getattr(item, stage)()
    for copy in sent:
        copy.wait_send()


def local(field_in, kernel_taps, row_reach, mix_weight, up_weight, down_weight, cotangent):
    total_points = points * lax.axis_size("lat") * lax.axis_size("lon")
    scale = 1.0 / math.sqrt(total_points)
    anywhere = pl.BlockSpec(memory_space=pl.ANY)
    v = pltpu.VMEM
    dma = pltpu.SemaphoreType.DMA
    resident = pl.BlockSpec(memory_space=pltpu.VMEM)
    shape = jax.ShapeDtypeStruct
    made = pl.pallas_call(
        lambda *refs: step_kernel(scale, *refs),
        out_shape=(
            shape(field_in.shape, bf16), shape(field_in.shape, bf16), shape((3584, lanes), bf16),
        ),
        in_specs=[anywhere] * 7,
        out_specs=(resident,) * 3,
        scratch_shapes=[
            v((rows + 2, wide, lanes), bf16),
            v((rows + 2, wide, lanes), bf16),
            v((rows, span, depth), bf16),
            v((rows, span, depth), bf16),
            v((basis, rows, 3, taps), bf16),
            pltpu.SMEM((rows,), jnp.int32),
            v((basis, rows + 2, 8, wide), f32),
            v((basis, rows + 2, 8, wide), f32),
            v((basis, points, lanes), bf16),
            v((rows, cols, lanes), bf16),
            v((points, lanes), bf16),
            v((points, hidden_units), f32),
            v((points, hidden_units), bf16),
            v((points, hidden_units), bf16),
            v((basis, lanes, lanes), bf16),
            v((lanes, hidden_units), bf16),
            v((hidden_units, lanes), bf16),
            v((3584, lanes), bf16),
            dma((7,)), dma((8,)), dma((8,)), dma((8,)), dma((8,)), dma((2,)), dma((2,)),
        ]
        + [part for start, count in stacks for part in Reduction.scratch(count)]
        + [dma((copies_each,)) for _ in range(2 * len(stacks))],
        compiler_params=pltpu.CompilerParams(
            collective_id=0, has_side_effects=True, vmem_limit_bytes=vmem_room
        ),
        name="disco_step",
    )(*[pltpu.with_memory_space_constraint(x, pltpu.HBM) for x in (field_in, kernel_taps, row_reach, mix_weight, up_weight, down_weight, cotangent)])
    return store_all(*[pltpu.with_memory_space_constraint(x, pltpu.VMEM) for x in made])


def store_kernel(block_rows, field_rows, total, block_out, field_out, mix_out, up_out, down_out, sem):
    stores = [
        pltpu.make_async_copy(block_rows, block_out, sem.at[0]),
        pltpu.make_async_copy(field_rows, field_out, sem.at[1]),
        pltpu.make_async_copy(total.at[0:512], up_out.at[:, 0:512], sem.at[2]),
        pltpu.make_async_copy(total.at[512:1024], up_out.at[:, 512:1024], sem.at[3]),
        pltpu.make_async_copy(total.at[1024:2048], down_out, sem.at[4]),
    ]
    for k in range(basis):
        stores.append(pltpu.make_async_copy(total.at[2048 + k * 512 : 2560 + k * 512], mix_out.at[k], sem.at[5 + k]))
    for store in stores:
        store.start()
    for store in stores:
        store.wait()


def store_all(block_rows, field_rows, total):
    shape = jax.ShapeDtypeStruct
    return pl.pallas_call(
        store_kernel,
        out_shape=(
            shape(block_rows.shape, bf16), shape(field_rows.shape, bf16), shape((basis, lanes, lanes), bf16),
            shape((lanes, hidden_units), bf16), shape((hidden_units, lanes), bf16),
        ),
        in_specs=[pl.BlockSpec(memory_space=pltpu.VMEM)] * 3,
        out_specs=(pl.BlockSpec(memory_space=pltpu.HBM),) * 5,
        scratch_shapes=[pltpu.SemaphoreType.DMA((8,))],
        compiler_params=pltpu.CompilerParams(vmem_limit_bytes=1024 * 1024),
        name="store_all",
    )(block_rows, field_rows, total)


def solution(mesh):
    placed = (
        P("lat", "lon", None),
        P(None, "lat", None, None),
        P("lat"),
        P(),
        P(),
        P(),
        P("lat", "lon", None),
    )
    return jax.shard_map(
        local,
        mesh=mesh,
        in_specs=placed,
        out_specs=(P("lat", "lon", None), P("lat", "lon", None), P(), P(), P()),
        check_vma=False,
    )
```

```python
import math

import jax
import jax.numpy as jnp
from jax import lax
from jax.experimental import pallas as pl
from jax.experimental.pallas import tpu as pltpu
from jax.sharding import PartitionSpec as P

inv_root_two = 0.7071067811865476
inv_root_tau = 0.3989422804014327

MESH = pl.DeviceIdType.MESH
ring_xy = 4
ring_z = 8
lanes = 512


def multiple(value, of):
    return pl.multiple_of(value, of)


def remote(src, dst, send_sem, recv_sem, device):
    return pltpu.make_async_remote_copy(
        src_ref=src, dst_ref=dst, send_sem=send_sem, recv_sem=recv_sem, device_id=device, device_id_type=MESH
    )


class Place:
    def __init__(self):
        self.lat = lax.axis_index("lat")
        self.lon = lax.axis_index("lon")
        self.z = lax.rem(self.lat, ring_z)
        self.core = lax.rem(self.lon, 2)
        self.y = lax.div(self.lon, 4)
        self.x = lax.rem(lax.div(self.lon, 2), 2) * 2 + lax.div(self.lat, ring_z)
        self.first = self.x * (1 - self.core) + self.y * self.core
        self.second = self.y * (1 - self.core) + self.x * self.core

    def device(self, x, y, z, core):
        return (lax.rem(x, 2) * ring_z + z, y * 4 + lax.div(x, 2) * 2 + core)

    def partner(self):
        return self.device(self.x, self.y, self.z, 1 - self.core)

    def along_x(self, step):
        return self.device(lax.rem(self.x + step, ring_xy), self.y, self.z, self.core)

    def along_y(self, step):
        return self.device(self.x, lax.rem(self.y + step, ring_xy), self.z, self.core)

    def along_z(self, step):
        return self.device(self.x, self.y, lax.rem(self.z + step, ring_z), self.core)

    def along_first(self, step):
        x = lax.rem(self.x + step * (1 - self.core), ring_xy)
        y = lax.rem(self.y + step * self.core, ring_xy)
        return self.device(x, y, self.z, self.core)

    def along_second(self, step):
        x = lax.rem(self.x + step * self.core, ring_xy)
        y = lax.rem(self.y + step * (1 - self.core), ring_xy)
        return self.device(x, y, self.z, self.core)

    def everyone(self):
        found = [self.partner()]
        found += [self.along_x(s) for s in range(1, ring_xy)]
        found += [self.along_y(s) for s in range(1, ring_xy)]
        found += [self.along_z(s) for s in range(1, ring_z)]
        return found


def add_rows(dst, dst_at, sources, count, chunk):
    def body(i, carry):
        total = None
        for ref, at in sources:
            term = ref[pl.ds(multiple(at + i * chunk, 16), chunk), :].astype(jnp.float32)
            total = term if total is None else total + term
        dst[pl.ds(multiple(dst_at + i * chunk, 16), chunk), :] = total.astype(dst.dtype)
        return carry

    lax.fori_loop(0, count // chunk, body, 0)


wire_steps = (2, 1, 3)
z_steps = (4, 3, 5, 2, 6, 1, 7)


class Reduction:
    def __init__(self, place, start, rows, grad, out, parts, send, recv, scale):
        self.p = place
        self.half, self.quarter, self.piece = rows // 2, rows // 8, rows // 32
        self.grad, self.out, self.scale = grad.at[start : start + rows], out.at[start : start + rows], scale
        self.r0, self.s0, self.r1, self.s1, self.r2, self.s2, self.r3, self.zbuf = parts
        self.send, self.recv = send, recv
        self.used = 0
        self.sent = []

    @staticmethod
    def scratch(rows):
        half, quarter, piece = rows // 2, rows // 8, rows // 32
        shapes = [
            (half, lanes), (half, lanes), (3, quarter, lanes), (quarter, lanes),
            (3, piece, lanes), (32, lanes), (7, 16, 128), (32, lanes),
        ]
        return [pltpu.VMEM(s, jnp.bfloat16) for s in shapes]

    def go(self, src, dst, device):
        copy = remote(src, dst, self.send.at[self.used], self.recv.at[self.used], device)
        self.used += 1
        copy.start()
        self.sent.append(copy)
        return copy

    def start_pair(self):
        p = self.p
        other = multiple((1 - p.core) * self.half, 16)
        self.flight = [self.go(self.grad.at[pl.ds(other, self.half), :], self.r0, p.partner())]

    def arrived(self):
        for copy in self.flight:
            copy.wait_recv()
        self.flight = []

    def block(self, ref, index, part):
        half = self.quarter // 2
        return ref.at[pl.ds(multiple(index * self.quarter + part * half, 16), half), :]

    def pair_then_first(self):
        p = self.p
        self.arrived()
        half = self.quarter // 2
        place = [lax.rem(p.first + step, ring_xy) for step in range(ring_xy)]

        def join(step):
            at = place[step] * self.quarter
            add_rows(self.s0, at, [(self.grad, p.core * self.half + at), (self.r0, at)], self.quarter, 64)

        top, low = self.r1.at[2, 0:half], self.r1.at[2, half : 2 * half]
        join(2)
        self.relayed = [
            self.go(self.block(self.s0, place[2], 0), top, p.along_first(1)),
            self.go(self.block(self.s0, place[2], 1), low, p.along_first(3)),
        ]
        join(1)
        self.flight = [self.go(self.block(self.s0, place[1], 1), self.r1.at[0, half : 2 * half], p.along_first(1))]
        join(3)
        self.flight.append(self.go(self.block(self.s0, place[3], 0), self.r1.at[1, 0:half], p.along_first(3)))
        join(0)

    def first_relay(self):
        p = self.p
        half = self.quarter // 2
        for copy, step, part in ((self.relayed[0], 1, 0), (self.relayed[1], 3, 1)):
            copy.wait_recv()
            index = lax.rem(p.first + step, ring_xy)
            at = index * self.quarter + part * half
            add_rows(self.s0, at, [(self.s0, at), (self.r1.at[2], part * half)], half, half)
            land = self.r1.at[0 if step == 1 else 1, part * half : part * half + half]
            self.flight.append(self.go(self.block(self.s0, index, part), land, p.along_first(step)))

    def first_then_second(self):
        p = self.p
        self.arrived()
        flight = []
        own = p.first * self.quarter
        for step in (2, 1, 3, 0):
            at = lax.rem(p.second + step, ring_xy) * self.piece
            sources = [(self.s0, own + at)] + [(self.r1.at[i], at) for i in range(2)]
            add_rows(self.s1, at, sources, self.piece, 16)
            if step:
                src = self.s1.at[pl.ds(multiple(at, 16), self.piece), :]
                flight.append(self.go(src, self.r2.at[step - 1], p.along_second(step)))
        self.flight = flight

    def spot(self, ref, index):
        row = multiple(lax.div(index, 4) * 16, 16)
        lane = multiple(lax.rem(index, 4) * 128, 128)
        return ref.at[pl.ds(row, 16), pl.ds(lane, 128)]

    def second_then_z(self):
        p = self.p
        self.arrived()
        sources = [(self.s1, p.second * self.piece)] + [(self.r2.at[i], 0) for i in range(3)]
        add_rows(self.s2, 0, sources, self.piece, 16)
        if self.piece < 32:
            self.s2[self.piece :, :] = jnp.zeros((32 - self.piece, lanes), jnp.bfloat16)
        flight = []
        for step in z_steps:
            src = self.spot(self.s2, lax.rem(p.z + step, ring_z))
            flight.append(self.go(src, self.r3.at[step - 1], p.along_z(step)))
        self.flight = flight

    def z_then_back(self):
        p = self.p
        self.arrived()
        total = self.spot(self.s2, p.z)[...].astype(jnp.float32)
        for i in range(7):
            total = total + self.r3[i].astype(jnp.float32)
        mine = self.spot(self.zbuf, p.z)
        mine[...] = (total * self.scale).astype(jnp.bfloat16)
        self.flight = [self.go(mine, mine, p.along_z(step)) for step in z_steps]

    def back_second(self):
        p = self.p
        self.arrived()
        at = p.core * self.half + p.first * self.quarter + p.second * self.piece
        mine = self.out.at[pl.ds(multiple(at, 16), self.piece), :]
        mine[...] = self.zbuf[: self.piece, :]
        self.flight = [self.go(mine, mine, p.along_second(step)) for step in wire_steps]

    def back_first(self):
        p = self.p
        self.arrived()
        mine = self.out.at[pl.ds(multiple(p.core * self.half, 16), self.half), :]
        parts = [self.block(mine, p.first, part) for part in range(2)]
        self.relayed = [self.go(parts[0], parts[0], p.along_first(1)), self.go(parts[1], parts[1], p.along_first(3))]
        self.flight = [self.go(parts[1], parts[1], p.along_first(1)), self.go(parts[0], parts[0], p.along_first(3))]
        quarter = mine.at[pl.ds(multiple(p.first * self.quarter, 16), self.quarter), :]
        self.handed = [self.go(quarter, quarter, p.partner())]

    def back_relay(self):
        p = self.p
        mine = self.out.at[pl.ds(multiple(p.core * self.half, 16), self.half), :]
        for copy, step, part in ((self.relayed[0], 1, 0), (self.relayed[1], 3, 1)):
            copy.wait_recv()
            came = self.block(mine, lax.rem(p.first + ring_xy - step, ring_xy), part)
            self.flight.append(self.go(came, came, p.along_first(step)))
            self.handed.append(self.go(came, came, p.partner()))

    def back_pair(self):
        p = self.p
        mine = self.out.at[pl.ds(multiple(p.core * self.half, 16), self.half), :]
        for copy, step, part in zip(self.flight, (3, 1, 2, 2), (1, 0, 0, 1)):
            copy.wait_recv()
            came = self.block(mine, lax.rem(p.first + step, ring_xy), part)
            self.handed.append(self.go(came, came, p.partner()))
        self.flight = self.handed

    def finish(self):
        self.arrived()
        for copy in self.sent:
            copy.wait_send()


copies_each = 40
stacks = ((0, 1024), (1024, 1024), (2048, 1024), (3072, 512))


rows = 10
cols = 96
reach = 16
vmem_room = 48 * 1024 * 1024
wide = cols + 2 * reach
taps = 2 * reach + 1
basis = 3
points = rows * cols
hidden_units = 1024
chunk_rows = 5
chunk = chunk_rows * cols
chunks = rows // chunk_rows
span = basis * cols
depth = 3 * wide
f32 = jnp.float32
bf16 = jnp.bfloat16


def mm(a, b):
    return jnp.dot(a, b, preferred_element_type=f32)


def mm_nt(a, b):
    return lax.dot_general(a, b, (((1,), (1,)), ((), ())), preferred_element_type=f32)


def mm_tn(a, b):
    return lax.dot_general(a, b, (((0,), (0,)), ((), ())), preferred_element_type=f32)


class Halo:
    def __init__(self, place):
        lat, lon = place.lat, place.lon
        top = (lat == 0).astype(jnp.int32)
        bottom = (lat == 15).astype(jnp.int32)
        self.top, self.bottom = top, bottom
        self.lat, self.lon = lat, lon
        self.north = lat - 1 + top
        self.south = lat + 1 - bottom
        self.side_n = 1 - top
        self.side_s = bottom

    def upper(self, shift):
        return (self.north, lax.rem(self.lon + 16 + shift + 8 * self.top, 16))

    def lower(self, shift):
        return (self.south, lax.rem(self.lon + 16 + shift + 8 * self.bottom, 16))

    def beside(self, shift):
        return (self.lat, lax.rem(self.lon + 16 + shift, 16))

    def everyone(self):
        return [self.upper(s) for s in (0, -1, 1)] + [self.lower(s) for s in (0, -1, 1)] + [self.beside(-1), self.beside(1)]

    def send(self, ext, send, recv):
        own = slice(reach, reach + cols)
        first, last = slice(reach, 2 * reach), slice(cols, cols + reach)
        left, right = slice(0, reach), slice(reach + cols, wide)
        copies = []
        copies.append(remote(ext.at[1 : rows + 1, first], ext.at[1 : rows + 1, right], send.at[6], recv.at[6], self.beside(-1)))
        copies.append(remote(ext.at[1 : rows + 1, last], ext.at[1 : rows + 1, left], send.at[7], recv.at[7], self.beside(1)))
        for number, (side, target, row) in enumerate(((self.side_n, self.upper, 1), (self.side_s, self.lower, rows))):
            to = side * (rows + 1)
            plan = ((own, own, 0), (first, right, -1), (last, left, 1))
            for part, (src, dst, shift) in enumerate(plan):
                copies.append(
                    remote(
                        ext.at[row, src], ext.at[to, dst], send.at[number * 3 + part], recv.at[side * 3 + part], target(shift)
                    )
                )
        for copy in copies:
            copy.start()
        return copies

    def wait_columns(self, ext, send, recv):
        me = self.beside(1)
        for number, first in ((6, reach + cols), (7, 0)):
            here = ext.at[1 : rows + 1, first : first + reach]
            remote(here, here, send.at[0], recv.at[number], me).wait_recv()

    def wait_rows(self, ext, send, recv):
        own = slice(reach, reach + cols)
        left, right = slice(0, reach), slice(reach + cols, wide)
        me = self.beside(1)
        for side in range(2):
            for part, where in enumerate((own, right, left)):
                here = ext.at[side * (rows + 1), where]
                remote(here, here, send.at[0], recv.at[side * 3 + part], me).wait_recv()


def toeplitz(row):
    spread = jnp.broadcast_to(row, (cols, wide))
    return pltpu.roll(spread, 0, 1, stride=1, stride_axis=0).astype(bf16)


def step_kernel(
    scale,
    field_in, taps_in, reach_in, mix_in, up_in, down_in, cot_in,
    block_rows, field_rows, total,
    ext, gext, band, adjoint, traw, far, tapx, revx, feats, cot, hidden, act_grad, act, pre_grad, mix, up, down,
    grads,
    load_sem, halo_send, halo_recv, grad_send, grad_recv, tap_send, tap_recv,
    *rest,
):
    place = Place()
    halo = Halo(place)
    own = slice(reach, reach + cols)

    loads = [
        pltpu.make_async_copy(taps_in, traw, load_sem.at[0]),
        pltpu.make_async_copy(reach_in, far, load_sem.at[6]),
        pltpu.make_async_copy(field_in, ext.at[1 : rows + 1, own], load_sem.at[1]),
        pltpu.make_async_copy(cot_in, cot, load_sem.at[2]),
        pltpu.make_async_copy(down_in, down, load_sem.at[3]),
        pltpu.make_async_copy(mix_in, mix, load_sem.at[4]),
        pltpu.make_async_copy(up_in, up, load_sem.at[5]),
    ]
    for load in loads:
        load.start()
    devices = place.everyone() + halo.everyone()
    barrier = pltpu.get_barrier_semaphore()
    for device in devices:
        pl.semaphore_signal(barrier, inc=1, device_id=device, device_id_type=MESH)

    loads[0].wait()

    loads[1].wait()
    tap_at = lax.broadcasted_iota(jnp.int32, (taps, 2 * wide), 0)
    spot_at = lax.broadcasted_iota(jnp.int32, (taps, 2 * wide), 1)
    select = ((spot_at == tap_at) | (spot_at == wide + taps - 1 - tap_at)).astype(f32).astype(bf16)
    away = jnp.abs(lax.broadcasted_iota(jnp.int32, (3, taps), 1) - reach)
    revx[:, 1 : rows + 1] = jnp.zeros((basis, rows, 8, wide), f32)

    def build(r, carry):
        for k in range(basis):
            kept = jnp.where(away <= far[r], traw[k, r].astype(f32), 0.0).astype(bf16)
            both = mm(kept, select)
            tapx[k, r + 1, 0:3, :] = both[:, :wide]
            revx[k, r + 1, 0:3, :] = both[:, wide:]
        for k in range(basis):
            for d in range(3):
                band[r, k * cols : (k + 1) * cols, d * wide : (d + 1) * wide] = toeplitz(
                    tapx[k, r + 1, d : d + 1, :]
                )
        return carry

    lax.fori_loop(0, rows, build, 0)
    loads[2].wait()
    pl.semaphore_wait(barrier, len(devices))
    sent = halo.send(ext, halo_send, halo_recv)
    tap_copies = [
        remote(revx.at[:, 1], revx.at[:, halo.side_n * (rows + 1)], tap_send.at[0], tap_recv.at[halo.side_n], halo.upper(0)),
        remote(revx.at[:, rows], revx.at[:, halo.side_s * (rows + 1)], tap_send.at[1], tap_recv.at[halo.side_s], halo.lower(0)),
    ]
    for copy in tap_copies:
        copy.start()
    sent += tap_copies

    loads[3].wait()
    loads[4].wait()

    def early(i, carry):
        at = pl.ds(multiple(i * chunk, 16), chunk)
        grad = cot[pl.ds(i * chunk_rows, chunk_rows)].reshape(chunk, lanes)
        act_grad[at, :] = mm_nt(grad, down[...])
        return carry

    lax.fori_loop(0, chunks, early, 0)

    def build_back(r, carry):
        for k in range(basis):
            for s in range(3):
                adjoint[r, k * cols : (k + 1) * cols, s * wide : (s + 1) * wide] = toeplitz(revx[k, r + s, 2 - s : 3 - s, :])
        return carry

    lax.fori_loop(1, rows - 1, build_back, 0)

    loads[5].wait()
    loads[6].wait()
    halo.wait_columns(ext, halo_send, halo_recv)

    def features(r, carry):
        window = ext[pl.ds(r, 3)].reshape(depth, lanes)
        made = mm(band[r], window).astype(bf16)
        at = pl.ds(multiple(r * cols, 16), cols)
        for k in range(basis):
            feats[k, at, :] = made[k * cols : (k + 1) * cols]
        return carry

    lax.fori_loop(1, rows - 1, features, 0)
    halo.wait_rows(ext, halo_send, halo_recv)
    features(0, 0)
    features(rows - 1, 0)

    def pointwise(i, carry):
        at = pl.ds(multiple(i * chunk, 16), chunk)
        total = ext[pl.ds(1 + i * chunk_rows, chunk_rows), own].reshape(chunk, lanes).astype(f32)
        for k in range(basis):
            total = total + mm(feats[k, at, :], mix[k])
        inner = total.astype(bf16)
        hidden[at, :] = inner
        for block in range(hidden_units // 256):
            f = slice(block * 256, (block + 1) * 256)
            value = mm(inner, up[:, f])
            cdf = 0.5 * (1.0 + lax.erf(value * inv_root_two))
            act[at, f] = (value * cdf).astype(bf16)
            slope = cdf + value * jnp.exp(-0.5 * value * value) * inv_root_tau
            pre_grad[at, f] = (act_grad[at, f] * slope).astype(bf16)
        made = (inner.astype(f32) + mm(act[at, :], down[...])).astype(bf16)
        block_rows[pl.ds(i * chunk_rows, chunk_rows)] = made.reshape(chunk_rows, cols, lanes)
        grad = cot[pl.ds(i * chunk_rows, chunk_rows)].reshape(chunk, lanes).astype(f32)
        grad = (grad + mm_nt(pre_grad[at, :], up[...])).astype(bf16)
        gext[pl.ds(1 + i * chunk_rows, chunk_rows), own] = grad.reshape(chunk_rows, cols, lanes)
        return carry

    lax.fori_loop(0, chunks, pointwise, 0)
    sent += halo.send(gext, grad_send, grad_recv)

    def flat(ref):
        return ref[...].reshape(points, lanes)

    sums = [
        Reduction(place, start, count, grads, total, rest[8 * n : 8 * n + 8], rest[32 + 2 * n], rest[33 + 2 * n], scale)
        for n, (start, count) in enumerate(stacks)
    ]
    sum_up, sum_down, sum_mix, sum_rest = sums

    def weight_down(i, carry):
        part = pl.ds(multiple(i * 256, 256), 256)
        grads[pl.ds(multiple(1024 + i * 256, 256), 256), :] = mm_tn(act[:, part], flat(cot)).astype(bf16)
        return carry

    lax.fori_loop(0, 4, weight_down, 0)
    sum_down.start_pair()

    def weight_up(i, carry):
        part = pl.ds(multiple(i * 256, 256), 256)
        left = hidden[:, part]
        for side in range(2):
            grads[pl.ds(multiple(side * 512 + i * 256, 256), 256), :] = mm_tn(
                left, pre_grad[:, side * 512 : side * 512 + 512]
            ).astype(bf16)
        return carry

    lax.fori_loop(0, 2, weight_up, 0)
    sum_up.start_pair()
    sum_down.pair_then_first()

    def weight_mix(i, carry):
        k, half = lax.div(i, 2), lax.rem(i, 2)
        part = pl.ds(multiple(half * 256, 256), 256)
        grad = gext[1 : rows + 1, own].reshape(points, lanes)
        grads[pl.ds(multiple(2048 + i * 256, 256), 256), :] = mm_tn(feats[k, :, part], grad).astype(bf16)
        return carry

    lax.fori_loop(0, 4, weight_mix, 0)
    sum_mix.start_pair()
    sum_up.pair_then_first()
    sum_down.first_relay()
    lax.fori_loop(4, 6, weight_mix, 0)
    sum_rest.start_pair()
    sum_mix.pair_then_first()
    sum_up.first_relay()

    for side in range(2):
        here = revx.at[:, side * (rows + 1)]
        remote(here, here, tap_send.at[0], tap_recv.at[side], halo.beside(1)).wait_recv()
    for r, pole in ((0, halo.top), (rows - 1, halo.bottom)):
        slot = 0 if r == 0 else rows + 1
        for k in range(basis):
            for s in range(3):
                row = revx[k, r + s, 2 - s : 3 - s, :]
                if r + s == slot:
                    row = jnp.where(pole == 1, revx[k, r + s, s : s + 1, :], row)
                adjoint[r, k * cols : (k + 1) * cols, s * wide : (s + 1) * wide] = toeplitz(row)

    def pull(r, carry):
        window = gext[pl.ds(r, 3)].reshape(depth, lanes)
        made = mm(adjoint[r], window).astype(bf16)
        at = pl.ds(multiple(r * cols, 16), cols)
        for k in range(basis):
            feats[k, at, :] = made[k * cols : (k + 1) * cols]
        return carry

    sum_rest.pair_then_first()
    sum_mix.first_relay()
    sum_rest.first_relay()
    sum_down.first_then_second()
    sum_up.first_then_second()
    halo.wait_columns(gext, grad_send, grad_recv)
    lax.fori_loop(1, 4, pull, 0)
    sum_mix.first_then_second()
    sum_rest.first_then_second()
    sum_down.second_then_z()
    sum_up.second_then_z()
    lax.fori_loop(4, rows - 1, pull, 0)
    halo.wait_rows(gext, grad_send, grad_recv)
    pull(0, 0)
    pull(rows - 1, 0)
    sum_mix.second_then_z()
    sum_rest.second_then_z()

    def last(i, carry):
        at = pl.ds(multiple(i * chunk, 16), chunk)
        made = gext[pl.ds(1 + i * chunk_rows, chunk_rows), own].reshape(chunk, lanes).astype(f32)
        for k in range(basis):
            made = made + mm_nt(feats[k, at, :], mix[k])
        field_rows[pl.ds(i * chunk_rows, chunk_rows)] = made.astype(bf16).reshape(chunk_rows, cols, lanes)
        return carry

    lax.fori_loop(0, 1, last, 0)
    order = (sum_down, sum_up, sum_mix, sum_rest)
    for item in order:
        item.z_then_back()
    lax.fori_loop(1, chunks, last, 0)
    for stage in ("back_second", "back_first", "back_relay", "back_pair", "finish"):
        for item in order:
            getattr(item, stage)()
    for copy in sent:
        copy.wait_send()


def local(field_in, kernel_taps, row_reach, mix_weight, up_weight, down_weight, cotangent):
    total_points = points * lax.axis_size("lat") * lax.axis_size("lon")
    scale = 1.0 / math.sqrt(total_points)
    anywhere = pl.BlockSpec(memory_space=pl.ANY)
    v = pltpu.VMEM
    dma = pltpu.SemaphoreType.DMA
    resident = pl.BlockSpec(memory_space=pltpu.VMEM)
    shape = jax.ShapeDtypeStruct
    made = pl.pallas_call(
        lambda *refs: step_kernel(scale, *refs),
        out_shape=(
            shape(field_in.shape, bf16), shape(field_in.shape, bf16), shape((3584, lanes), bf16),
        ),
        in_specs=[anywhere] * 7,
        out_specs=(resident,) * 3,
        scratch_shapes=[
            v((rows + 2, wide, lanes), bf16),
            v((rows + 2, wide, lanes), bf16),
            v((rows, span, depth), bf16),
            v((rows, span, depth), bf16),
            v((basis, rows, 3, taps), bf16),
            pltpu.SMEM((rows,), jnp.int32),
            v((basis, rows + 2, 8, wide), f32),
            v((basis, rows + 2, 8, wide), f32),
            v((basis, points, lanes), bf16),
            v((rows, cols, lanes), bf16),
            v((points, lanes), bf16),
            v((points, hidden_units), f32),
            v((points, hidden_units), bf16),
            v((points, hidden_units), bf16),
            v((basis, lanes, lanes), bf16),
            v((lanes, hidden_units), bf16),
            v((hidden_units, lanes), bf16),
            v((3584, lanes), bf16),
            dma((7,)), dma((8,)), dma((8,)), dma((8,)), dma((8,)), dma((2,)), dma((2,)),
        ]
        + [part for start, count in stacks for part in Reduction.scratch(count)]
        + [dma((copies_each,)) for _ in range(2 * len(stacks))],
        compiler_params=pltpu.CompilerParams(
            collective_id=0, has_side_effects=True, vmem_limit_bytes=vmem_room
        ),
        name="disco_step",
    )(*[pltpu.with_memory_space_constraint(x, pltpu.HBM) for x in (field_in, kernel_taps, row_reach, mix_weight, up_weight, down_weight, cotangent)])
    return store_all(*[pltpu.with_memory_space_constraint(x, pltpu.VMEM) for x in made])


def store_kernel(block_rows, field_rows, total, block_out, field_out, mix_out, up_out, down_out, sem):
    stores = [
        pltpu.make_async_copy(block_rows, block_out, sem.at[0]),
        pltpu.make_async_copy(field_rows, field_out, sem.at[1]),
        pltpu.make_async_copy(total.at[0:512], up_out.at[:, 0:512], sem.at[2]),
        pltpu.make_async_copy(total.at[512:1024], up_out.at[:, 512:1024], sem.at[3]),
        pltpu.make_async_copy(total.at[1024:2048], down_out, sem.at[4]),
    ]
    for k in range(basis):
        stores.append(pltpu.make_async_copy(total.at[2048 + k * 512 : 2560 + k * 512], mix_out.at[k], sem.at[5 + k]))
    for store in stores:
        store.start()
    for store in stores:
        store.wait()


def store_all(block_rows, field_rows, total):
    shape = jax.ShapeDtypeStruct
    return pl.pallas_call(
        store_kernel,
        out_shape=(
            shape(block_rows.shape, bf16), shape(field_rows.shape, bf16), shape((basis, lanes, lanes), bf16),
            shape((lanes, hidden_units), bf16), shape((hidden_units, lanes), bf16),
        ),
        in_specs=[pl.BlockSpec(memory_space=pltpu.VMEM)] * 3,
        out_specs=(pl.BlockSpec(memory_space=pltpu.HBM),) * 5,
        scratch_shapes=[pltpu.SemaphoreType.DMA((8,))],
        compiler_params=pltpu.CompilerParams(vmem_limit_bytes=1024 * 1024),
        name="store_all",
    )(block_rows, field_rows, total)


def solution(mesh):
    placed = (
        P("lat", "lon", None),
        P(None, "lat", None, None),
        P("lat"),
        P(),
        P(),
        P(),
        P("lat", "lon", None),
    )
    return jax.shard_map(
        local,
        mesh=mesh,
        in_specs=placed,
        out_specs=(P("lat", "lon", None), P("lat", "lon", None), P(), P(), P()),
        check_vma=False,
    )
```

```python
import math

import jax
import jax.numpy as jnp
from jax import lax
from jax.experimental import pallas as pl
from jax.experimental.pallas import tpu as pltpu
from jax.sharding import PartitionSpec as P

inv_root_two = 0.7071067811865476
inv_root_tau = 0.3989422804014327

MESH = pl.DeviceIdType.MESH
ring_xy = 4
ring_z = 8
lanes = 512


def multiple(value, of):
    return pl.multiple_of(value, of)


def remote(src, dst, send_sem, recv_sem, device):
    return pltpu.make_async_remote_copy(
        src_ref=src, dst_ref=dst, send_sem=send_sem, recv_sem=recv_sem, device_id=device, device_id_type=MESH
    )


class Place:
    def __init__(self):
        self.lat = lax.axis_index("lat")
        self.lon = lax.axis_index("lon")
        self.z = lax.rem(self.lat, ring_z)
        self.core = lax.rem(self.lon, 2)
        self.y = lax.div(self.lon, 4)
        self.x = lax.rem(lax.div(self.lon, 2), 2) * 2 + lax.div(self.lat, ring_z)
        self.first = self.x * (1 - self.core) + self.y * self.core
        self.second = self.y * (1 - self.core) + self.x * self.core

    def device(self, x, y, z, core):
        return (lax.rem(x, 2) * ring_z + z, y * 4 + lax.div(x, 2) * 2 + core)

    def partner(self):
        return self.device(self.x, self.y, self.z, 1 - self.core)

    def along_x(self, step):
        return self.device(lax.rem(self.x + step, ring_xy), self.y, self.z, self.core)

    def along_y(self, step):
        return self.device(self.x, lax.rem(self.y + step, ring_xy), self.z, self.core)

    def along_z(self, step):
        return self.device(self.x, self.y, lax.rem(self.z + step, ring_z), self.core)

    def along_first(self, step):
        x = lax.rem(self.x + step * (1 - self.core), ring_xy)
        y = lax.rem(self.y + step * self.core, ring_xy)
        return self.device(x, y, self.z, self.core)

    def along_second(self, step):
        x = lax.rem(self.x + step * self.core, ring_xy)
        y = lax.rem(self.y + step * (1 - self.core), ring_xy)
        return self.device(x, y, self.z, self.core)

    def everyone(self):
        found = [self.partner()]
        found += [self.along_x(s) for s in range(1, ring_xy)]
        found += [self.along_y(s) for s in range(1, ring_xy)]
        found += [self.along_z(s) for s in range(1, ring_z)]
        return found


def add_rows(dst, dst_at, sources, count, chunk):
    def body(i, carry):
        total = None
        for ref, at in sources:
            term = ref[pl.ds(multiple(at + i * chunk, 16), chunk), :].astype(jnp.float32)
            total = term if total is None else total + term
        dst[pl.ds(multiple(dst_at + i * chunk, 16), chunk), :] = total.astype(dst.dtype)
        return carry

    lax.fori_loop(0, count // chunk, body, 0)


wire_steps = (2, 1, 3)
z_steps = (4, 3, 5, 2, 6, 1, 7)


class Reduction:
    def __init__(self, place, start, rows, grad, out, parts, send, recv, scale):
        self.p = place
        self.half, self.quarter, self.piece = rows // 2, rows // 8, rows // 32
        self.grad, self.out, self.scale = grad.at[start : start + rows], out.at[start : start + rows], scale
        self.r0, self.s0, self.r1, self.s1, self.r2, self.s2, self.r3, self.zbuf = parts
        self.send, self.recv = send, recv
        self.used = 0
        self.sent = []

    @staticmethod
    def scratch(rows):
        half, quarter, piece = rows // 2, rows // 8, rows // 32
        shapes = [
            (half, lanes), (half, lanes), (3, quarter, lanes), (quarter, lanes),
            (3, piece, lanes), (32, lanes), (7, 16, 128), (32, lanes),
        ]
        return [pltpu.VMEM(s, jnp.bfloat16) for s in shapes]

    def go(self, src, dst, device):
        copy = remote(src, dst, self.send.at[self.used], self.recv.at[self.used], device)
        self.used += 1
        copy.start()
        self.sent.append(copy)
        return copy

    def start_pair(self):
        p = self.p
        other = multiple((1 - p.core) * self.half, 16)
        self.flight = [self.go(self.grad.at[pl.ds(other, self.half), :], self.r0, p.partner())]

    def arrived(self):
        for copy in self.flight:
            copy.wait_recv()
        self.flight = []

    def block(self, ref, index, part):
        half = self.quarter // 2
        return ref.at[pl.ds(multiple(index * self.quarter + part * half, 16), half), :]

    def pair_then_first(self):
        p = self.p
        self.arrived()
        half = self.quarter // 2
        place = [lax.rem(p.first + step, ring_xy) for step in range(ring_xy)]

        def join(step):
            at = place[step] * self.quarter
            add_rows(self.s0, at, [(self.grad, p.core * self.half + at), (self.r0, at)], self.quarter, 64)

        top, low = self.r1.at[2, 0:half], self.r1.at[2, half : 2 * half]
        join(2)
        self.relayed = [
            self.go(self.block(self.s0, place[2], 0), top, p.along_first(1)),
            self.go(self.block(self.s0, place[2], 1), low, p.along_first(3)),
        ]
        join(1)
        self.flight = [self.go(self.block(self.s0, place[1], 1), self.r1.at[0, half : 2 * half], p.along_first(1))]
        join(3)
        self.flight.append(self.go(self.block(self.s0, place[3], 0), self.r1.at[1, 0:half], p.along_first(3)))
        join(0)

    def first_relay(self):
        p = self.p
        half = self.quarter // 2
        for copy, step, part in ((self.relayed[0], 1, 0), (self.relayed[1], 3, 1)):
            copy.wait_recv()
            index = lax.rem(p.first + step, ring_xy)
            at = index * self.quarter + part * half
            add_rows(self.s0, at, [(self.s0, at), (self.r1.at[2], part * half)], half, half)
            land = self.r1.at[0 if step == 1 else 1, part * half : part * half + half]
            self.flight.append(self.go(self.block(self.s0, index, part), land, p.along_first(step)))

    def first_then_second(self):
        p = self.p
        self.arrived()
        flight = []
        own = p.first * self.quarter
        for step in (2, 1, 3, 0):
            at = lax.rem(p.second + step, ring_xy) * self.piece
            sources = [(self.s0, own + at)] + [(self.r1.at[i], at) for i in range(2)]
            add_rows(self.s1, at, sources, self.piece, 16)
            if step:
                src = self.s1.at[pl.ds(multiple(at, 16), self.piece), :]
                flight.append(self.go(src, self.r2.at[step - 1], p.along_second(step)))
        self.flight = flight

    def spot(self, ref, index):
        row = multiple(lax.div(index, 4) * 16, 16)
        lane = multiple(lax.rem(index, 4) * 128, 128)
        return ref.at[pl.ds(row, 16), pl.ds(lane, 128)]

    def second_then_z(self):
        p = self.p
        self.arrived()
        sources = [(self.s1, p.second * self.piece)] + [(self.r2.at[i], 0) for i in range(3)]
        add_rows(self.s2, 0, sources, self.piece, 16)
        if self.piece < 32:
            self.s2[self.piece :, :] = jnp.zeros((32 - self.piece, lanes), jnp.bfloat16)
        flight = []
        for step in z_steps:
            src = self.spot(self.s2, lax.rem(p.z + step, ring_z))
            flight.append(self.go(src, self.r3.at[step - 1], p.along_z(step)))
        self.flight = flight

    def z_then_back(self):
        p = self.p
        self.arrived()
        total = self.spot(self.s2, p.z)[...].astype(jnp.float32)
        for i in range(7):
            total = total + self.r3[i].astype(jnp.float32)
        mine = self.spot(self.zbuf, p.z)
        mine[...] = (total * self.scale).astype(jnp.bfloat16)
        self.flight = [self.go(mine, mine, p.along_z(step)) for step in z_steps]

    def back_second(self):
        p = self.p
        self.arrived()
        at = p.core * self.half + p.first * self.quarter + p.second * self.piece
        mine = self.out.at[pl.ds(multiple(at, 16), self.piece), :]
        mine[...] = self.zbuf[: self.piece, :]
        self.flight = [self.go(mine, mine, p.along_second(step)) for step in wire_steps]

    def back_first(self):
        p = self.p
        self.arrived()
        mine = self.out.at[pl.ds(multiple(p.core * self.half, 16), self.half), :]
        parts = [self.block(mine, p.first, part) for part in range(2)]
        self.relayed = [self.go(parts[0], parts[0], p.along_first(1)), self.go(parts[1], parts[1], p.along_first(3))]
        self.flight = [self.go(parts[1], parts[1], p.along_first(1)), self.go(parts[0], parts[0], p.along_first(3))]
        quarter = mine.at[pl.ds(multiple(p.first * self.quarter, 16), self.quarter), :]
        self.handed = [self.go(quarter, quarter, p.partner())]

    def back_relay(self):
        p = self.p
        mine = self.out.at[pl.ds(multiple(p.core * self.half, 16), self.half), :]
        for copy, step, part in ((self.relayed[0], 1, 0), (self.relayed[1], 3, 1)):
            copy.wait_recv()
            came = self.block(mine, lax.rem(p.first + ring_xy - step, ring_xy), part)
            self.flight.append(self.go(came, came, p.along_first(step)))
            self.handed.append(self.go(came, came, p.partner()))

    def back_pair(self):
        p = self.p
        mine = self.out.at[pl.ds(multiple(p.core * self.half, 16), self.half), :]
        for copy, step, part in zip(self.flight, (3, 1, 2, 2), (1, 0, 0, 1)):
            copy.wait_recv()
            came = self.block(mine, lax.rem(p.first + step, ring_xy), part)
            self.handed.append(self.go(came, came, p.partner()))
        self.flight = self.handed

    def finish(self):
        self.arrived()
        for copy in self.sent:
            copy.wait_send()


copies_each = 40
stacks = ((0, 1024), (1024, 1024), (2048, 1024), (3072, 512))


rows = 10
cols = 96
reach = 16
vmem_room = 48 * 1024 * 1024
wide = cols + 2 * reach
taps = 2 * reach + 1
basis = 3
points = rows * cols
hidden_units = 1024
chunk_rows = 5
chunk = chunk_rows * cols
chunks = rows // chunk_rows
span = basis * cols
depth = 3 * wide
f32 = jnp.float32
bf16 = jnp.bfloat16


def mm(a, b):
    return jnp.dot(a, b, preferred_element_type=f32)


def mm_nt(a, b):
    return lax.dot_general(a, b, (((1,), (1,)), ((), ())), preferred_element_type=f32)


def mm_tn(a, b):
    return lax.dot_general(a, b, (((0,), (0,)), ((), ())), preferred_element_type=f32)


class Halo:
    def __init__(self, place):
        lat, lon = place.lat, place.lon
        top = (lat == 0).astype(jnp.int32)
        bottom = (lat == 15).astype(jnp.int32)
        self.top, self.bottom = top, bottom
        self.lat, self.lon = lat, lon
        self.north = lat - 1 + top
        self.south = lat + 1 - bottom
        self.side_n = 1 - top
        self.side_s = bottom

    def upper(self, shift):
        return (self.north, lax.rem(self.lon + 16 + shift + 8 * self.top, 16))

    def lower(self, shift):
        return (self.south, lax.rem(self.lon + 16 + shift + 8 * self.bottom, 16))

    def beside(self, shift):
        return (self.lat, lax.rem(self.lon + 16 + shift, 16))

    def everyone(self):
        return [self.upper(s) for s in (0, -1, 1)] + [self.lower(s) for s in (0, -1, 1)] + [self.beside(-1), self.beside(1)]

    def send(self, ext, send, recv):
        own = slice(reach, reach + cols)
        first, last = slice(reach, 2 * reach), slice(cols, cols + reach)
        left, right = slice(0, reach), slice(reach + cols, wide)
        copies = []
        copies.append(remote(ext.at[1 : rows + 1, first], ext.at[1 : rows + 1, right], send.at[6], recv.at[6], self.beside(-1)))
        copies.append(remote(ext.at[1 : rows + 1, last], ext.at[1 : rows + 1, left], send.at[7], recv.at[7], self.beside(1)))
        for number, (side, target, row) in enumerate(((self.side_n, self.upper, 1), (self.side_s, self.lower, rows))):
            to = side * (rows + 1)
            plan = ((own, own, 0), (first, right, -1), (last, left, 1))
            for part, (src, dst, shift) in enumerate(plan):
                copies.append(
                    remote(
                        ext.at[row, src], ext.at[to, dst], send.at[number * 3 + part], recv.at[side * 3 + part], target(shift)
                    )
                )
        for copy in copies:
            copy.start()
        return copies

    def wait_columns(self, ext, send, recv):
        me = self.beside(1)
        for number, first in ((6, reach + cols), (7, 0)):
            here = ext.at[1 : rows + 1, first : first + reach]
            remote(here, here, send.at[0], recv.at[number], me).wait_recv()

    def wait_rows(self, ext, send, recv):
        own = slice(reach, reach + cols)
        left, right = slice(0, reach), slice(reach + cols, wide)
        me = self.beside(1)
        for side in range(2):
            for part, where in enumerate((own, right, left)):
                here = ext.at[side * (rows + 1), where]
                remote(here, here, send.at[0], recv.at[side * 3 + part], me).wait_recv()


def toeplitz(row):
    spread = jnp.broadcast_to(row, (cols, wide))
    return pltpu.roll(spread, 0, 1, stride=1, stride_axis=0).astype(bf16)


def step_kernel(
    scale,
    field_in, taps_in, reach_in, mix_in, up_in, down_in, cot_in,
    block_rows, field_rows, total,
    ext, gext, band, adjoint, traw, far, tapx, revx, feats, cot, hidden, act_grad, act, pre_grad, mix, up, down,
    grads,
    load_sem, halo_send, halo_recv, grad_send, grad_recv, tap_send, tap_recv,
    *rest,
):
    place = Place()
    halo = Halo(place)
    own = slice(reach, reach + cols)

    loads = [
        pltpu.make_async_copy(taps_in, traw, load_sem.at[0]),
        pltpu.make_async_copy(reach_in, far, load_sem.at[6]),
        pltpu.make_async_copy(field_in, ext.at[1 : rows + 1, own], load_sem.at[1]),
        pltpu.make_async_copy(cot_in, cot, load_sem.at[2]),
        pltpu.make_async_copy(down_in, down, load_sem.at[3]),
        pltpu.make_async_copy(mix_in, mix, load_sem.at[4]),
        pltpu.make_async_copy(up_in, up, load_sem.at[5]),
    ]
    for load in loads:
        load.start()
    devices = place.everyone() + halo.everyone()
    barrier = pltpu.get_barrier_semaphore()
    for device in devices:
        pl.semaphore_signal(barrier, inc=1, device_id=device, device_id_type=MESH)

    loads[0].wait()

    loads[1].wait()
    tap_at = lax.broadcasted_iota(jnp.int32, (taps, 2 * wide), 0)
    spot_at = lax.broadcasted_iota(jnp.int32, (taps, 2 * wide), 1)
    select = ((spot_at == tap_at) | (spot_at == wide + taps - 1 - tap_at)).astype(f32).astype(bf16)
    away = jnp.abs(lax.broadcasted_iota(jnp.int32, (3, taps), 1) - reach)
    revx[:, 1 : rows + 1] = jnp.zeros((basis, rows, 8, wide), f32)

    def build(r, carry):
        for k in range(basis):
            kept = jnp.where(away <= far[r], traw[k, r].astype(f32), 0.0).astype(bf16)
            both = mm(kept, select)
            tapx[k, r + 1, 0:3, :] = both[:, :wide]
            revx[k, r + 1, 0:3, :] = both[:, wide:]
        for k in range(basis):
            for d in range(3):
                band[r, k * cols : (k + 1) * cols, d * wide : (d + 1) * wide] = toeplitz(
                    tapx[k, r + 1, d : d + 1, :]
                )
        return carry

    lax.fori_loop(0, rows, build, 0)
    loads[2].wait()
    pl.semaphore_wait(barrier, len(devices))
    sent = halo.send(ext, halo_send, halo_recv)
    tap_copies = [
        remote(revx.at[:, 1], revx.at[:, halo.side_n * (rows + 1)], tap_send.at[0], tap_recv.at[halo.side_n], halo.upper(0)),
        remote(revx.at[:, rows], revx.at[:, halo.side_s * (rows + 1)], tap_send.at[1], tap_recv.at[halo.side_s], halo.lower(0)),
    ]
    for copy in tap_copies:
        copy.start()
    sent += tap_copies

    loads[3].wait()
    loads[4].wait()

    def early(i, carry):
        at = pl.ds(multiple(i * chunk, 16), chunk)
        grad = cot[pl.ds(i * chunk_rows, chunk_rows)].reshape(chunk, lanes)
        act_grad[at, :] = mm_nt(grad, down[...])
        return carry

    lax.fori_loop(0, chunks, early, 0)

    def build_back(r, carry):
        for k in range(basis):
            for s in range(3):
                adjoint[r, k * cols : (k + 1) * cols, s * wide : (s + 1) * wide] = toeplitz(revx[k, r + s, 2 - s : 3 - s, :])
        return carry

    lax.fori_loop(1, rows - 1, build_back, 0)

    loads[5].wait()
    loads[6].wait()
    halo.wait_columns(ext, halo_send, halo_recv)

    def features(r, carry):
        window = ext[pl.ds(r, 3)].reshape(depth, lanes)
        made = mm(band[r], window).astype(bf16)
        at = pl.ds(multiple(r * cols, 16), cols)
        for k in range(basis):
            feats[k, at, :] = made[k * cols : (k + 1) * cols]
        return carry

    lax.fori_loop(1, rows - 1, features, 0)
    halo.wait_rows(ext, halo_send, halo_recv)
    features(0, 0)
    features(rows - 1, 0)

    def pointwise(i, carry):
        at = pl.ds(multiple(i * chunk, 16), chunk)
        total = ext[pl.ds(1 + i * chunk_rows, chunk_rows), own].reshape(chunk, lanes).astype(f32)
        for k in range(basis):
            total = total + mm(feats[k, at, :], mix[k])
        inner = total.astype(bf16)
        hidden[at, :] = inner
        for block in range(hidden_units // 256):
            f = slice(block * 256, (block + 1) * 256)
            value = mm(inner, up[:, f])
            cdf = 0.5 * (1.0 + lax.erf(value * inv_root_two))
            act[at, f] = (value * cdf).astype(bf16)
            slope = cdf + value * jnp.exp(-0.5 * value * value) * inv_root_tau
            pre_grad[at, f] = (act_grad[at, f] * slope).astype(bf16)
        made = (inner.astype(f32) + mm(act[at, :], down[...])).astype(bf16)
        block_rows[pl.ds(i * chunk_rows, chunk_rows)] = made.reshape(chunk_rows, cols, lanes)
        grad = cot[pl.ds(i * chunk_rows, chunk_rows)].reshape(chunk, lanes).astype(f32)
        grad = (grad + mm_nt(pre_grad[at, :], up[...])).astype(bf16)
        gext[pl.ds(1 + i * chunk_rows, chunk_rows), own] = grad.reshape(chunk_rows, cols, lanes)
        return carry

    lax.fori_loop(0, chunks, pointwise, 0)
    sent += halo.send(gext, grad_send, grad_recv)

    def flat(ref):
        return ref[...].reshape(points, lanes)

    sums = [
        Reduction(place, start, count, grads, total, rest[8 * n : 8 * n + 8], rest[32 + 2 * n], rest[33 + 2 * n], scale)
        for n, (start, count) in enumerate(stacks)
    ]
    sum_up, sum_down, sum_mix, sum_rest = sums

    def weight_down(i, carry):
        part = pl.ds(multiple(i * 512, 512), 512)
        grads[pl.ds(multiple(1024 + i * 512, 512), 512), :] = mm_tn(act[:, part], flat(cot)).astype(bf16)
        return carry

    lax.fori_loop(0, 2, weight_down, 0)
    sum_down.start_pair()

    def weight_up(i, carry):
        part = pl.ds(multiple(i * 256, 256), 256)
        left = hidden[:, part]
        for side in range(2):
            grads[pl.ds(multiple(side * 512 + i * 256, 256), 256), :] = mm_tn(
                left, pre_grad[:, side * 512 : side * 512 + 512]
            ).astype(bf16)
        return carry

    lax.fori_loop(0, 2, weight_up, 0)
    sum_up.start_pair()
    sum_down.pair_then_first()

    def weight_mix(i, carry):
        grad = gext[1 : rows + 1, own].reshape(points, lanes)
        grads[pl.ds(multiple(2048 + i * 512, 512), 512), :] = mm_tn(feats[i], grad).astype(bf16)
        return carry

    lax.fori_loop(0, 2, weight_mix, 0)
    sum_mix.start_pair()
    sum_up.pair_then_first()
    sum_down.first_relay()
    lax.fori_loop(2, 3, weight_mix, 0)
    sum_rest.start_pair()
    sum_mix.pair_then_first()
    sum_up.first_relay()

    for side in range(2):
        here = revx.at[:, side * (rows + 1)]
        remote(here, here, tap_send.at[0], tap_recv.at[side], halo.beside(1)).wait_recv()
    for r, pole in ((0, halo.top), (rows - 1, halo.bottom)):
        slot = 0 if r == 0 else rows + 1
        for k in range(basis):
            for s in range(3):
                row = revx[k, r + s, 2 - s : 3 - s, :]
                if r + s == slot:
                    row = jnp.where(pole == 1, revx[k, r + s, s : s + 1, :], row)
                adjoint[r, k * cols : (k + 1) * cols, s * wide : (s + 1) * wide] = toeplitz(row)

    def pull(r, carry):
        window = gext[pl.ds(r, 3)].reshape(depth, lanes)
        made = mm(adjoint[r], window).astype(bf16)
        at = pl.ds(multiple(r * cols, 16), cols)
        for k in range(basis):
            feats[k, at, :] = made[k * cols : (k + 1) * cols]
        return carry

    sum_rest.pair_then_first()
    sum_mix.first_relay()
    sum_rest.first_relay()
    sum_down.first_then_second()
    sum_up.first_then_second()
    halo.wait_columns(gext, grad_send, grad_recv)
    lax.fori_loop(1, 4, pull, 0)
    sum_mix.first_then_second()
    sum_rest.first_then_second()
    sum_down.second_then_z()
    sum_up.second_then_z()
    lax.fori_loop(4, rows - 1, pull, 0)
    halo.wait_rows(gext, grad_send, grad_recv)
    pull(0, 0)
    pull(rows - 1, 0)
    sum_mix.second_then_z()
    sum_rest.second_then_z()

    def last(i, carry):
        at = pl.ds(multiple(i * chunk, 16), chunk)
        made = gext[pl.ds(1 + i * chunk_rows, chunk_rows), own].reshape(chunk, lanes).astype(f32)
        for k in range(basis):
            made = made + mm_nt(feats[k, at, :], mix[k])
        field_rows[pl.ds(i * chunk_rows, chunk_rows)] = made.astype(bf16).reshape(chunk_rows, cols, lanes)
        return carry

    lax.fori_loop(0, 1, last, 0)
    order = (sum_down, sum_up, sum_mix, sum_rest)
    for item in order:
        item.z_then_back()
    lax.fori_loop(1, chunks, last, 0)
    for stage in ("back_second", "back_first", "back_relay", "back_pair", "finish"):
        for item in order:
            getattr(item, stage)()
    for copy in sent:
        copy.wait_send()


def local(field_in, kernel_taps, row_reach, mix_weight, up_weight, down_weight, cotangent):
    total_points = points * lax.axis_size("lat") * lax.axis_size("lon")
    scale = 1.0 / math.sqrt(total_points)
    anywhere = pl.BlockSpec(memory_space=pl.ANY)
    v = pltpu.VMEM
    dma = pltpu.SemaphoreType.DMA
    resident = pl.BlockSpec(memory_space=pltpu.VMEM)
    shape = jax.ShapeDtypeStruct
    made = pl.pallas_call(
        lambda *refs: step_kernel(scale, *refs),
        out_shape=(
            shape(field_in.shape, bf16), shape(field_in.shape, bf16), shape((3584, lanes), bf16),
        ),
        in_specs=[anywhere] * 7,
        out_specs=(resident,) * 3,
        scratch_shapes=[
            v((rows + 2, wide, lanes), bf16),
            v((rows + 2, wide, lanes), bf16),
            v((rows, span, depth), bf16),
            v((rows, span, depth), bf16),
            v((basis, rows, 3, taps), bf16),
            pltpu.SMEM((rows,), jnp.int32),
            v((basis, rows + 2, 8, wide), f32),
            v((basis, rows + 2, 8, wide), f32),
            v((basis, points, lanes), bf16),
            v((rows, cols, lanes), bf16),
            v((points, lanes), bf16),
            v((points, hidden_units), f32),
            v((points, hidden_units), bf16),
            v((points, hidden_units), bf16),
            v((basis, lanes, lanes), bf16),
            v((lanes, hidden_units), bf16),
            v((hidden_units, lanes), bf16),
            v((3584, lanes), bf16),
            dma((7,)), dma((8,)), dma((8,)), dma((8,)), dma((8,)), dma((2,)), dma((2,)),
        ]
        + [part for start, count in stacks for part in Reduction.scratch(count)]
        + [dma((copies_each,)) for _ in range(2 * len(stacks))],
        compiler_params=pltpu.CompilerParams(
            collective_id=0, has_side_effects=True, vmem_limit_bytes=vmem_room
        ),
        name="disco_step",
    )(*[pltpu.with_memory_space_constraint(x, pltpu.HBM) for x in (field_in, kernel_taps, row_reach, mix_weight, up_weight, down_weight, cotangent)])
    return store_all(*[pltpu.with_memory_space_constraint(x, pltpu.VMEM) for x in made])


def store_kernel(block_rows, field_rows, total, block_out, field_out, mix_out, up_out, down_out, sem):
    stores = [
        pltpu.make_async_copy(block_rows, block_out, sem.at[0]),
        pltpu.make_async_copy(field_rows, field_out, sem.at[1]),
        pltpu.make_async_copy(total.at[0:512], up_out.at[:, 0:512], sem.at[2]),
        pltpu.make_async_copy(total.at[512:1024], up_out.at[:, 512:1024], sem.at[3]),
        pltpu.make_async_copy(total.at[1024:2048], down_out, sem.at[4]),
    ]
    for k in range(basis):
        stores.append(pltpu.make_async_copy(total.at[2048 + k * 512 : 2560 + k * 512], mix_out.at[k], sem.at[5 + k]))
    for store in stores:
        store.start()
    for store in stores:
        store.wait()


def store_all(block_rows, field_rows, total):
    shape = jax.ShapeDtypeStruct
    return pl.pallas_call(
        store_kernel,
        out_shape=(
            shape(block_rows.shape, bf16), shape(field_rows.shape, bf16), shape((basis, lanes, lanes), bf16),
            shape((lanes, hidden_units), bf16), shape((hidden_units, lanes), bf16),
        ),
        in_specs=[pl.BlockSpec(memory_space=pltpu.VMEM)] * 3,
        out_specs=(pl.BlockSpec(memory_space=pltpu.HBM),) * 5,
        scratch_shapes=[pltpu.SemaphoreType.DMA((8,))],
        compiler_params=pltpu.CompilerParams(vmem_limit_bytes=1024 * 1024),
        name="store_all",
    )(block_rows, field_rows, total)


def solution(mesh):
    placed = (
        P("lat", "lon", None),
        P(None, "lat", None, None),
        P("lat"),
        P(),
        P(),
        P(),
        P("lat", "lon", None),
    )
    return jax.shard_map(
        local,
        mesh=mesh,
        in_specs=placed,
        out_specs=(P("lat", "lon", None), P("lat", "lon", None), P(), P(), P()),
        check_vma=False,
    )
```

```python
import math

import jax
import jax.numpy as jnp
from jax import lax
from jax.experimental import pallas as pl
from jax.experimental.pallas import tpu as pltpu
from jax.sharding import PartitionSpec as P

inv_root_two = 0.7071067811865476
inv_root_tau = 0.3989422804014327

MESH = pl.DeviceIdType.MESH
ring_xy = 4
ring_z = 8
lanes = 512


def multiple(value, of):
    return pl.multiple_of(value, of)


def remote(src, dst, send_sem, recv_sem, device):
    return pltpu.make_async_remote_copy(
        src_ref=src, dst_ref=dst, send_sem=send_sem, recv_sem=recv_sem, device_id=device, device_id_type=MESH
    )


class Place:
    def __init__(self):
        self.lat = lax.axis_index("lat")
        self.lon = lax.axis_index("lon")
        self.z = lax.rem(self.lat, ring_z)
        self.core = lax.rem(self.lon, 2)
        self.y = lax.div(self.lon, 4)
        self.x = lax.rem(lax.div(self.lon, 2), 2) * 2 + lax.div(self.lat, ring_z)
        self.first = self.x * (1 - self.core) + self.y * self.core
        self.second = self.y * (1 - self.core) + self.x * self.core

    def device(self, x, y, z, core):
        return (lax.rem(x, 2) * ring_z + z, y * 4 + lax.div(x, 2) * 2 + core)

    def partner(self):
        return self.device(self.x, self.y, self.z, 1 - self.core)

    def along_x(self, step):
        return self.device(lax.rem(self.x + step, ring_xy), self.y, self.z, self.core)

    def along_y(self, step):
        return self.device(self.x, lax.rem(self.y + step, ring_xy), self.z, self.core)

    def along_z(self, step):
        return self.device(self.x, self.y, lax.rem(self.z + step, ring_z), self.core)

    def along_first(self, step):
        x = lax.rem(self.x + step * (1 - self.core), ring_xy)
        y = lax.rem(self.y + step * self.core, ring_xy)
        return self.device(x, y, self.z, self.core)

    def along_second(self, step):
        x = lax.rem(self.x + step * self.core, ring_xy)
        y = lax.rem(self.y + step * (1 - self.core), ring_xy)
        return self.device(x, y, self.z, self.core)

    def everyone(self):
        found = [self.partner()]
        found += [self.along_x(s) for s in range(1, ring_xy)]
        found += [self.along_y(s) for s in range(1, ring_xy)]
        found += [self.along_z(s) for s in range(1, ring_z)]
        return found


def add_rows(dst, dst_at, sources, count, chunk):
    def body(i, carry):
        total = None
        for ref, at in sources:
            term = ref[pl.ds(multiple(at + i * chunk, 16), chunk), :].astype(jnp.float32)
            total = term if total is None else total + term
        dst[pl.ds(multiple(dst_at + i * chunk, 16), chunk), :] = total.astype(dst.dtype)
        return carry

    lax.fori_loop(0, count // chunk, body, 0)


wire_steps = (2, 1, 3)
z_steps = (4, 3, 5, 2, 6, 1, 7)


class Reduction:
    def __init__(self, place, start, rows, grad, out, parts, send, recv, scale):
        self.p = place
        self.half, self.quarter, self.piece = rows // 2, rows // 8, rows // 32
        self.grad, self.out, self.scale = grad.at[start : start + rows], out.at[start : start + rows], scale
        self.r0, self.s0, self.r1, self.s1, self.r2, self.s2, self.r3, self.zbuf = parts
        self.send, self.recv = send, recv
        self.used = 0
        self.sent = []

    @staticmethod
    def scratch(rows):
        half, quarter, piece = rows // 2, rows // 8, rows // 32
        shapes = [
            (half, lanes), (half, lanes), (3, quarter, lanes), (quarter, lanes),
            (3, piece, lanes), (32, lanes), (7, 16, 128), (32, lanes),
        ]
        return [pltpu.VMEM(s, jnp.bfloat16) for s in shapes]

    def go(self, src, dst, device):
        copy = remote(src, dst, self.send.at[self.used], self.recv.at[self.used], device)
        self.used += 1
        copy.start()
        self.sent.append(copy)
        return copy

    def start_pair(self):
        p = self.p
        other = multiple((1 - p.core) * self.half, 16)
        self.flight = [self.go(self.grad.at[pl.ds(other, self.half), :], self.r0, p.partner())]

    def arrived(self):
        for copy in self.flight:
            copy.wait_recv()
        self.flight = []

    def block(self, ref, index, part):
        half = self.quarter // 2
        return ref.at[pl.ds(multiple(index * self.quarter + part * half, 16), half), :]

    def pair_then_first(self):
        p = self.p
        self.arrived()
        half = self.quarter // 2
        place = [lax.rem(p.first + step, ring_xy) for step in range(ring_xy)]

        def join(step):
            at = place[step] * self.quarter
            add_rows(self.s0, at, [(self.grad, p.core * self.half + at), (self.r0, at)], self.quarter, 64)

        top, low = self.r1.at[2, 0:half], self.r1.at[2, half : 2 * half]
        join(2)
        self.relayed = [
            self.go(self.block(self.s0, place[2], 0), top, p.along_first(1)),
            self.go(self.block(self.s0, place[2], 1), low, p.along_first(3)),
        ]
        join(1)
        self.flight = [self.go(self.block(self.s0, place[1], 1), self.r1.at[0, half : 2 * half], p.along_first(1))]
        join(3)
        self.flight.append(self.go(self.block(self.s0, place[3], 0), self.r1.at[1, 0:half], p.along_first(3)))
        join(0)

    def first_relay(self):
        p = self.p
        half = self.quarter // 2
        for copy, step, part in ((self.relayed[0], 1, 0), (self.relayed[1], 3, 1)):
            copy.wait_recv()
            index = lax.rem(p.first + step, ring_xy)
            at = index * self.quarter + part * half
            add_rows(self.s0, at, [(self.s0, at), (self.r1.at[2], part * half)], half, half)
            land = self.r1.at[0 if step == 1 else 1, part * half : part * half + half]
            self.flight.append(self.go(self.block(self.s0, index, part), land, p.along_first(step)))

    def first_then_second(self):
        p = self.p
        self.arrived()
        flight = []
        own = p.first * self.quarter
        for step in (2, 1, 3, 0):
            at = lax.rem(p.second + step, ring_xy) * self.piece
            sources = [(self.s0, own + at)] + [(self.r1.at[i], at) for i in range(2)]
            add_rows(self.s1, at, sources, self.piece, 16)
            if step:
                src = self.s1.at[pl.ds(multiple(at, 16), self.piece), :]
                flight.append(self.go(src, self.r2.at[step - 1], p.along_second(step)))
        self.flight = flight

    def spot(self, ref, index):
        row = multiple(lax.div(index, 4) * 16, 16)
        lane = multiple(lax.rem(index, 4) * 128, 128)
        return ref.at[pl.ds(row, 16), pl.ds(lane, 128)]

    def second_then_z(self):
        p = self.p
        self.arrived()
        sources = [(self.s1, p.second * self.piece)] + [(self.r2.at[i], 0) for i in range(3)]
        add_rows(self.s2, 0, sources, self.piece, 16)
        if self.piece < 32:
            self.s2[self.piece :, :] = jnp.zeros((32 - self.piece, lanes), jnp.bfloat16)
        flight = []
        for step in z_steps:
            src = self.spot(self.s2, lax.rem(p.z + step, ring_z))
            flight.append(self.go(src, self.r3.at[step - 1], p.along_z(step)))
        self.flight = flight

    def z_then_back(self):
        p = self.p
        self.arrived()
        total = self.spot(self.s2, p.z)[...].astype(jnp.float32)
        for i in range(7):
            total = total + self.r3[i].astype(jnp.float32)
        mine = self.spot(self.zbuf, p.z)
        mine[...] = (total * self.scale).astype(jnp.bfloat16)
        self.flight = [self.go(mine, mine, p.along_z(step)) for step in z_steps]

    def back_second(self):
        p = self.p
        self.arrived()
        at = p.core * self.half + p.first * self.quarter + p.second * self.piece
        mine = self.out.at[pl.ds(multiple(at, 16), self.piece), :]
        mine[...] = self.zbuf[: self.piece, :]
        self.flight = [self.go(mine, mine, p.along_second(step)) for step in wire_steps]

    def back_first(self):
        p = self.p
        self.arrived()
        mine = self.out.at[pl.ds(multiple(p.core * self.half, 16), self.half), :]
        parts = [self.block(mine, p.first, part) for part in range(2)]
        self.relayed = [self.go(parts[0], parts[0], p.along_first(1)), self.go(parts[1], parts[1], p.along_first(3))]
        self.flight = [self.go(parts[1], parts[1], p.along_first(1)), self.go(parts[0], parts[0], p.along_first(3))]
        quarter = mine.at[pl.ds(multiple(p.first * self.quarter, 16), self.quarter), :]
        self.handed = [self.go(quarter, quarter, p.partner())]

    def back_relay(self):
        p = self.p
        mine = self.out.at[pl.ds(multiple(p.core * self.half, 16), self.half), :]
        for copy, step, part in ((self.relayed[0], 1, 0), (self.relayed[1], 3, 1)):
            copy.wait_recv()
            came = self.block(mine, lax.rem(p.first + ring_xy - step, ring_xy), part)
            self.flight.append(self.go(came, came, p.along_first(step)))
            self.handed.append(self.go(came, came, p.partner()))

    def back_pair(self):
        p = self.p
        mine = self.out.at[pl.ds(multiple(p.core * self.half, 16), self.half), :]
        for copy, step, part in zip(self.flight, (3, 1, 2, 2), (1, 0, 0, 1)):
            copy.wait_recv()
            came = self.block(mine, lax.rem(p.first + step, ring_xy), part)
            self.handed.append(self.go(came, came, p.partner()))
        self.flight = self.handed

    def finish(self):
        self.arrived()
        for copy in self.sent:
            copy.wait_send()


copies_each = 40
stacks = ((0, 1024), (1024, 1024), (2048, 1024), (3072, 512))


rows = 10
cols = 96
reach = 16
vmem_room = 48 * 1024 * 1024
wide = cols + 2 * reach
taps = 2 * reach + 1
basis = 3
points = rows * cols
hidden_units = 1024
chunk_rows = 5
chunk = chunk_rows * cols
chunks = rows // chunk_rows
span = basis * cols
depth = 3 * wide
f32 = jnp.float32
bf16 = jnp.bfloat16


def mm(a, b):
    return jnp.dot(a, b, preferred_element_type=f32)


def mm_nt(a, b):
    return lax.dot_general(a, b, (((1,), (1,)), ((), ())), preferred_element_type=f32)


def mm_tn(a, b):
    return lax.dot_general(a, b, (((0,), (0,)), ((), ())), preferred_element_type=f32)


class Halo:
    def __init__(self, place):
        lat, lon = place.lat, place.lon
        top = (lat == 0).astype(jnp.int32)
        bottom = (lat == 15).astype(jnp.int32)
        self.top, self.bottom = top, bottom
        self.lat, self.lon = lat, lon
        self.north = lat - 1 + top
        self.south = lat + 1 - bottom
        self.side_n = 1 - top
        self.side_s = bottom

    def upper(self, shift):
        return (self.north, lax.rem(self.lon + 16 + shift + 8 * self.top, 16))

    def lower(self, shift):
        return (self.south, lax.rem(self.lon + 16 + shift + 8 * self.bottom, 16))

    def beside(self, shift):
        return (self.lat, lax.rem(self.lon + 16 + shift, 16))

    def everyone(self):
        return [self.upper(s) for s in (0, -1, 1)] + [self.lower(s) for s in (0, -1, 1)] + [self.beside(-1), self.beside(1)]

    def send(self, ext, send, recv):
        own = slice(reach, reach + cols)
        first, last = slice(reach, 2 * reach), slice(cols, cols + reach)
        left, right = slice(0, reach), slice(reach + cols, wide)
        copies = []
        copies.append(remote(ext.at[1 : rows + 1, first], ext.at[1 : rows + 1, right], send.at[6], recv.at[6], self.beside(-1)))
        copies.append(remote(ext.at[1 : rows + 1, last], ext.at[1 : rows + 1, left], send.at[7], recv.at[7], self.beside(1)))
        for number, (side, target, row) in enumerate(((self.side_n, self.upper, 1), (self.side_s, self.lower, rows))):
            to = side * (rows + 1)
            plan = ((own, own, 0), (first, right, -1), (last, left, 1))
            for part, (src, dst, shift) in enumerate(plan):
                copies.append(
                    remote(
                        ext.at[row, src], ext.at[to, dst], send.at[number * 3 + part], recv.at[side * 3 + part], target(shift)
                    )
                )
        for copy in copies:
            copy.start()
        return copies

    def wait_columns(self, ext, send, recv):
        me = self.beside(1)
        for number, first in ((6, reach + cols), (7, 0)):
            here = ext.at[1 : rows + 1, first : first + reach]
            remote(here, here, send.at[0], recv.at[number], me).wait_recv()

    def wait_rows(self, ext, send, recv):
        own = slice(reach, reach + cols)
        left, right = slice(0, reach), slice(reach + cols, wide)
        me = self.beside(1)
        for side in range(2):
            for part, where in enumerate((own, right, left)):
                here = ext.at[side * (rows + 1), where]
                remote(here, here, send.at[0], recv.at[side * 3 + part], me).wait_recv()


def toeplitz(row):
    spread = jnp.broadcast_to(row, (cols, wide))
    return pltpu.roll(spread, 0, 1, stride=1, stride_axis=0).astype(bf16)


def step_kernel(
    scale,
    field_in, taps_in, reach_in, mix_in, up_in, down_in, cot_in,
    block_rows, field_rows, total,
    ext, gext, band, adjoint, traw, far, tapx, revx, feats, cot, hidden, act_grad, act, pre_grad, mix, up, down,
    grads,
    load_sem, halo_send, halo_recv, grad_send, grad_recv, tap_send, tap_recv,
    *rest,
):
    place = Place()
    halo = Halo(place)
    own = slice(reach, reach + cols)

    loads = [
        pltpu.make_async_copy(taps_in, traw, load_sem.at[0]),
        pltpu.make_async_copy(reach_in, far, load_sem.at[6]),
        pltpu.make_async_copy(field_in, ext.at[1 : rows + 1, own], load_sem.at[1]),
        pltpu.make_async_copy(cot_in, cot, load_sem.at[2]),
        pltpu.make_async_copy(down_in, down, load_sem.at[3]),
        pltpu.make_async_copy(mix_in, mix, load_sem.at[4]),
        pltpu.make_async_copy(up_in, up, load_sem.at[5]),
    ]
    for load in loads:
        load.start()
    devices = place.everyone() + halo.everyone()
    barrier = pltpu.get_barrier_semaphore()
    for device in devices:
        pl.semaphore_signal(barrier, inc=1, device_id=device, device_id_type=MESH)

    loads[0].wait()

    loads[1].wait()
    tap_at = lax.broadcasted_iota(jnp.int32, (taps, 2 * wide), 0)
    spot_at = lax.broadcasted_iota(jnp.int32, (taps, 2 * wide), 1)
    select = ((spot_at == tap_at) | (spot_at == wide + taps - 1 - tap_at)).astype(f32).astype(bf16)
    away = jnp.abs(lax.broadcasted_iota(jnp.int32, (3, taps), 1) - reach)
    revx[:, 1 : rows + 1] = jnp.zeros((basis, rows, 8, wide), f32)

    def build(r, carry):
        for k in range(basis):
            kept = jnp.where(away <= far[r], traw[k, r].astype(f32), 0.0).astype(bf16)
            both = mm(kept, select)
            tapx[k, r + 1, 0:3, :] = both[:, :wide]
            revx[k, r + 1, 0:3, :] = both[:, wide:]
        for k in range(basis):
            for d in range(3):
                band[r, k * cols : (k + 1) * cols, d * wide : (d + 1) * wide] = toeplitz(
                    tapx[k, r + 1, d : d + 1, :]
                )
        return carry

    lax.fori_loop(0, 5, build, 0)
    loads[2].wait()
    pl.semaphore_wait(barrier, len(devices))
    sent = halo.send(ext, halo_send, halo_recv)
    lax.fori_loop(5, rows, build, 0)
    tap_copies = [
        remote(revx.at[:, 1], revx.at[:, halo.side_n * (rows + 1)], tap_send.at[0], tap_recv.at[halo.side_n], halo.upper(0)),
        remote(revx.at[:, rows], revx.at[:, halo.side_s * (rows + 1)], tap_send.at[1], tap_recv.at[halo.side_s], halo.lower(0)),
    ]
    for copy in tap_copies:
        copy.start()
    sent += tap_copies

    loads[3].wait()
    loads[4].wait()

    def early(i, carry):
        at = pl.ds(multiple(i * chunk, 16), chunk)
        grad = cot[pl.ds(i * chunk_rows, chunk_rows)].reshape(chunk, lanes)
        act_grad[at, :] = mm_nt(grad, down[...])
        return carry

    lax.fori_loop(0, chunks, early, 0)

    def build_back(r, carry):
        for k in range(basis):
            for s in range(3):
                adjoint[r, k * cols : (k + 1) * cols, s * wide : (s + 1) * wide] = toeplitz(revx[k, r + s, 2 - s : 3 - s, :])
        return carry

    lax.fori_loop(1, rows - 1, build_back, 0)

    loads[5].wait()
    loads[6].wait()
    halo.wait_columns(ext, halo_send, halo_recv)

    def features(r, carry):
        window = ext[pl.ds(r, 3)].reshape(depth, lanes)
        made = mm(band[r], window).astype(bf16)
        at = pl.ds(multiple(r * cols, 16), cols)
        for k in range(basis):
            feats[k, at, :] = made[k * cols : (k + 1) * cols]
        return carry

    lax.fori_loop(1, rows - 1, features, 0)
    halo.wait_rows(ext, halo_send, halo_recv)
    features(0, 0)
    features(rows - 1, 0)

    def pointwise(i, carry):
        at = pl.ds(multiple(i * chunk, 16), chunk)
        total = ext[pl.ds(1 + i * chunk_rows, chunk_rows), own].reshape(chunk, lanes).astype(f32)
        for k in range(basis):
            total = total + mm(feats[k, at, :], mix[k])
        inner = total.astype(bf16)
        hidden[at, :] = inner
        for block in range(hidden_units // 256):
            f = slice(block * 256, (block + 1) * 256)
            value = mm(inner, up[:, f])
            cdf = 0.5 * (1.0 + lax.erf(value * inv_root_two))
            act[at, f] = (value * cdf).astype(bf16)
            slope = cdf + value * jnp.exp(-0.5 * value * value) * inv_root_tau
            pre_grad[at, f] = (act_grad[at, f] * slope).astype(bf16)
        made = (inner.astype(f32) + mm(act[at, :], down[...])).astype(bf16)
        block_rows[pl.ds(i * chunk_rows, chunk_rows)] = made.reshape(chunk_rows, cols, lanes)
        grad = cot[pl.ds(i * chunk_rows, chunk_rows)].reshape(chunk, lanes).astype(f32)
        grad = (grad + mm_nt(pre_grad[at, :], up[...])).astype(bf16)
        gext[pl.ds(1 + i * chunk_rows, chunk_rows), own] = grad.reshape(chunk_rows, cols, lanes)
        return carry

    lax.fori_loop(0, chunks, pointwise, 0)
    sent += halo.send(gext, grad_send, grad_recv)

    def flat(ref):
        return ref[...].reshape(points, lanes)

    sums = [
        Reduction(place, start, count, grads, total, rest[8 * n : 8 * n + 8], rest[32 + 2 * n], rest[33 + 2 * n], scale)
        for n, (start, count) in enumerate(stacks)
    ]
    sum_up, sum_down, sum_mix, sum_rest = sums

    def weight_down(i, carry):
        part = pl.ds(multiple(i * 512, 512), 512)
        grads[pl.ds(multiple(1024 + i * 512, 512), 512), :] = mm_tn(act[:, part], flat(cot)).astype(bf16)
        return carry

    lax.fori_loop(0, 2, weight_down, 0)
    sum_down.start_pair()

    def weight_up(i, carry):
        part = pl.ds(multiple(i * 256, 256), 256)
        left = hidden[:, part]
        for side in range(2):
            grads[pl.ds(multiple(side * 512 + i * 256, 256), 256), :] = mm_tn(
                left, pre_grad[:, side * 512 : side * 512 + 512]
            ).astype(bf16)
        return carry

    lax.fori_loop(0, 2, weight_up, 0)
    sum_up.start_pair()
    sum_down.pair_then_first()

    def weight_mix(i, carry):
        grad = gext[1 : rows + 1, own].reshape(points, lanes)
        grads[pl.ds(multiple(2048 + i * 512, 512), 512), :] = mm_tn(feats[i], grad).astype(bf16)
        return carry

    lax.fori_loop(0, 2, weight_mix, 0)
    sum_mix.start_pair()
    sum_up.pair_then_first()
    sum_down.first_relay()
    lax.fori_loop(2, 3, weight_mix, 0)
    sum_rest.start_pair()
    sum_mix.pair_then_first()
    sum_up.first_relay()

    for side in range(2):
        here = revx.at[:, side * (rows + 1)]
        remote(here, here, tap_send.at[0], tap_recv.at[side], halo.beside(1)).wait_recv()
    for r, pole in ((0, halo.top), (rows - 1, halo.bottom)):
        slot = 0 if r == 0 else rows + 1
        for k in range(basis):
            for s in range(3):
                row = revx[k, r + s, 2 - s : 3 - s, :]
                if r + s == slot:
                    row = jnp.where(pole == 1, revx[k, r + s, s : s + 1, :], row)
                adjoint[r, k * cols : (k + 1) * cols, s * wide : (s + 1) * wide] = toeplitz(row)

    def pull(r, carry):
        window = gext[pl.ds(r, 3)].reshape(depth, lanes)
        made = mm(adjoint[r], window).astype(bf16)
        at = pl.ds(multiple(r * cols, 16), cols)
        for k in range(basis):
            feats[k, at, :] = made[k * cols : (k + 1) * cols]
        return carry

    sum_rest.pair_then_first()
    sum_mix.first_relay()
    sum_rest.first_relay()
    sum_down.first_then_second()
    sum_up.first_then_second()
    halo.wait_columns(gext, grad_send, grad_recv)
    lax.fori_loop(1, 4, pull, 0)
    sum_mix.first_then_second()
    sum_rest.first_then_second()
    sum_down.second_then_z()
    sum_up.second_then_z()
    lax.fori_loop(4, rows - 1, pull, 0)
    halo.wait_rows(gext, grad_send, grad_recv)
    pull(0, 0)
    pull(rows - 1, 0)
    sum_mix.second_then_z()
    sum_rest.second_then_z()

    def last(i, carry):
        at = pl.ds(multiple(i * chunk, 16), chunk)
        made = gext[pl.ds(1 + i * chunk_rows, chunk_rows), own].reshape(chunk, lanes).astype(f32)
        for k in range(basis):
            made = made + mm_nt(feats[k, at, :], mix[k])
        field_rows[pl.ds(i * chunk_rows, chunk_rows)] = made.astype(bf16).reshape(chunk_rows, cols, lanes)
        return carry

    lax.fori_loop(0, 1, last, 0)
    order = (sum_down, sum_up, sum_mix, sum_rest)
    for item in order:
        item.z_then_back()
    lax.fori_loop(1, chunks, last, 0)
    for stage in ("back_second", "back_first", "back_relay", "back_pair", "finish"):
        for item in order:
            getattr(item, stage)()
    for copy in sent:
        copy.wait_send()


def local(field_in, kernel_taps, row_reach, mix_weight, up_weight, down_weight, cotangent):
    total_points = points * lax.axis_size("lat") * lax.axis_size("lon")
    scale = 1.0 / math.sqrt(total_points)
    anywhere = pl.BlockSpec(memory_space=pl.ANY)
    v = pltpu.VMEM
    dma = pltpu.SemaphoreType.DMA
    resident = pl.BlockSpec(memory_space=pltpu.VMEM)
    shape = jax.ShapeDtypeStruct
    made = pl.pallas_call(
        lambda *refs: step_kernel(scale, *refs),
        out_shape=(
            shape(field_in.shape, bf16), shape(field_in.shape, bf16), shape((3584, lanes), bf16),
        ),
        in_specs=[anywhere] * 7,
        out_specs=(resident,) * 3,
        scratch_shapes=[
            v((rows + 2, wide, lanes), bf16),
            v((rows + 2, wide, lanes), bf16),
            v((rows, span, depth), bf16),
            v((rows, span, depth), bf16),
            v((basis, rows, 3, taps), bf16),
            pltpu.SMEM((rows,), jnp.int32),
            v((basis, rows + 2, 8, wide), f32),
            v((basis, rows + 2, 8, wide), f32),
            v((basis, points, lanes), bf16),
            v((rows, cols, lanes), bf16),
            v((points, lanes), bf16),
            v((points, hidden_units), f32),
            v((points, hidden_units), bf16),
            v((points, hidden_units), bf16),
            v((basis, lanes, lanes), bf16),
            v((lanes, hidden_units), bf16),
            v((hidden_units, lanes), bf16),
            v((3584, lanes), bf16),
            dma((7,)), dma((8,)), dma((8,)), dma((8,)), dma((8,)), dma((2,)), dma((2,)),
        ]
        + [part for start, count in stacks for part in Reduction.scratch(count)]
        + [dma((copies_each,)) for _ in range(2 * len(stacks))],
        compiler_params=pltpu.CompilerParams(
            collective_id=0, has_side_effects=True, vmem_limit_bytes=vmem_room
        ),
        name="disco_step",
    )(*[pltpu.with_memory_space_constraint(x, pltpu.HBM) for x in (field_in, kernel_taps, row_reach, mix_weight, up_weight, down_weight, cotangent)])
    return store_all(*[pltpu.with_memory_space_constraint(x, pltpu.VMEM) for x in made])


def store_kernel(block_rows, field_rows, total, block_out, field_out, mix_out, up_out, down_out, sem):
    stores = [
        pltpu.make_async_copy(block_rows, block_out, sem.at[0]),
        pltpu.make_async_copy(field_rows, field_out, sem.at[1]),
        pltpu.make_async_copy(total.at[0:512], up_out.at[:, 0:512], sem.at[2]),
        pltpu.make_async_copy(total.at[512:1024], up_out.at[:, 512:1024], sem.at[3]),
        pltpu.make_async_copy(total.at[1024:2048], down_out, sem.at[4]),
    ]
    for k in range(basis):
        stores.append(pltpu.make_async_copy(total.at[2048 + k * 512 : 2560 + k * 512], mix_out.at[k], sem.at[5 + k]))
    for store in stores:
        store.start()
    for store in stores:
        store.wait()


def store_all(block_rows, field_rows, total):
    shape = jax.ShapeDtypeStruct
    return pl.pallas_call(
        store_kernel,
        out_shape=(
            shape(block_rows.shape, bf16), shape(field_rows.shape, bf16), shape((basis, lanes, lanes), bf16),
            shape((lanes, hidden_units), bf16), shape((hidden_units, lanes), bf16),
        ),
        in_specs=[pl.BlockSpec(memory_space=pltpu.VMEM)] * 3,
        out_specs=(pl.BlockSpec(memory_space=pltpu.HBM),) * 5,
        scratch_shapes=[pltpu.SemaphoreType.DMA((8,))],
        compiler_params=pltpu.CompilerParams(vmem_limit_bytes=1024 * 1024),
        name="store_all",
    )(block_rows, field_rows, total)


def solution(mesh):
    placed = (
        P("lat", "lon", None),
        P(None, "lat", None, None),
        P("lat"),
        P(),
        P(),
        P(),
        P("lat", "lon", None),
    )
    return jax.shard_map(
        local,
        mesh=mesh,
        in_specs=placed,
        out_specs=(P("lat", "lon", None), P("lat", "lon", None), P(), P(), P()),
        check_vma=False,
    )
```
